32 devices in a mesh: wide: 4 (over z), narrow: 8 (over y, x, core).
Axes of the slice: x: 2, y: 2, z: 4, core: 2. Of those that a mesh axis runs over, the one named last changes fastest.
Arguments:
- sources: bfloat16 [32768, 768], P(('wide', 'narrow')), as said below
- targets: bfloat16 [32768, 768], P(('wide', 'narrow')), as said below
- target_lists: int32 [256, 4], P(('wide', 'narrow')), may hold values from 0 to 255, as said below
- target_clusters: int32 [32768], P(('wide', 'narrow')), may hold values from 0 to 8191
- centroids_src: bfloat16 [8192, 768], P(('wide', 'narrow')), may hold values from -6 to 6
- centroids_tgt: bfloat16 [8192, 768], P('narrow', 'wide'), may hold values from -6 to 6
- sender_mean_measure: float32 [8192], P('wide'), may hold values from 0.05 to 20
- recipient_mean_measure: float32 [8192], P('narrow'), may hold values from 0.05 to 20
Outputs:
- src_bary: bfloat16 [32768, 768], P(('wide', 'narrow'))
- tgt_bary: bfloat16 [32768, 768], P(('wide', 'narrow'))
- src_potential: float32 [32768], P(('wide', 'narrow'))
- tgt_potential: float32 [32768], P(('wide', 'narrow'))
The draws below stay inside these ranges and needn't reach their ends.
Inputs may be any that keep to these rules, and one draw needn't show every extreme that they name: `target_lists`: target block t holds targets t * 128 to (t + 1) * 128 - 1. Every entry names a block held by a device with the same wide index as the device of the source block. Among the 32 entries of one device, at most 5 name blocks held by any one device, and on every device some device is named by exactly 5. Every target block is named by at least one entry. `sources`: Real-valued features. `targets`: Real-valued features.
All inputs are finite; a program needn't handle non-finite values.
Results may differ from the reference program's by a relative error of at most 0.007.
Values may be sent and summed in bfloat16 or wider, within the bound.
A program may use at most 128 MiB of HBM per device.

```python
import math
import jax
import jax.numpy as jnp
from jax import lax

D = 768
KC = 8192
BLK = 128
LIST = 4
ITC = 6
STEPS = 3
NB_DEV = 8
TB_DEV = 8
CAP = 5
NBLK = 256
NS = 32768
NT = 32768
N_NARROW = 8


def feature_rows(key, row_count):
    values = jax.random.normal(key, (row_count, D), jnp.float32)
    return values.astype(jnp.bfloat16)


def draw_sources(key, part):
    return feature_rows(jax.random.fold_in(key, 101), NS)


def draw_targets(key, part):
    return feature_rows(jax.random.fold_in(key, 202), NT)


def draw_target_lists(key, part):
    device_count = NBLK // NB_DEV
    pool_size = N_NARROW * CAP
    entry_count = NB_DEV * LIST
    shifts = jax.random.randint(jax.random.fold_in(key, 7), (device_count // N_NARROW,), 0, N_NARROW)

    def one_device(device):
        device_key = jax.random.fold_in(key, device + 11)
        first_key, second_key, third_key = jax.random.split(device_key, 3)
        wide_index = device // N_NARROW
        narrow_index = device % N_NARROW
        pool_index = jnp.arange(pool_size)
        owner_of = pool_index // CAP
        copy_of = pool_index % CAP
        relative = (owner_of - narrow_index - shifts[wide_index]) % N_NARROW
        block_cover = relative + N_NARROW * copy_of
        covering = block_cover < TB_DEV
        forced = jnp.logical_or(covering, relative == 0)
        order_key = jax.random.permutation(first_key, pool_size)
        rank_of = jnp.zeros((pool_size,), jnp.int32).at[order_key].set(pool_index.astype(jnp.int32))
        score = jnp.where(forced, 0, 1) * pool_size + rank_of
        chosen = jnp.argsort(score)[:entry_count]
        random_local = jax.random.randint(second_key, (pool_size,), 0, TB_DEV)
        local_block = jnp.where(covering, block_cover, random_local)
        block_ids = (wide_index * N_NARROW + owner_of) * TB_DEV + local_block
        picked = block_ids[chosen]
        placed = picked[jax.random.permutation(third_key, entry_count)]
        return placed.reshape(NB_DEV, LIST)
    return jax.vmap(one_device)(jnp.arange(device_count)).reshape(NBLK, LIST).astype(jnp.int32)


def place_ends(array, own_key, smallest, largest):
    extent = array.shape
    spot = [jax.random.randint(jax.random.fold_in(own_key, axis), (), 0, extent[axis]) for axis in range(len(extent))]
    array = array.at[tuple(spot)].set(smallest)
    longest = extent.index(max(extent))
    spot[longest] = (spot[longest] + 1) % extent[longest]
    return array.at[tuple(spot)].set(largest)


def levels(own_key, shape, cuts, least, high):
    factor_of, own = 1.0, jax.random.fold_in(own_key, 6)
    for axis_at, blocks in cuts:
        heights = jnp.exp(jax.random.uniform(jax.random.fold_in(own, axis_at), (blocks,), jnp.float32, least / len(cuts), high / len(cuts)))
        factor_of = factor_of * jnp.repeat(heights, shape[axis_at] // blocks).reshape([-1 if axis == axis_at else 1 for axis in range(len(shape))])
    return factor_of


def centred(own_key, extent, spread, limit, pieces=(), dtype=jnp.bfloat16):
    level = levels(own_key, extent, pieces, -0.22, 0.18) if pieces else 1.0
    drawn = jax.random.normal(own_key, extent, jnp.float32) * spread * level
    return jnp.minimum(jnp.maximum(drawn, -limit), limit).astype(dtype)


def setup_inputs(seed: int = 0) -> dict:
    seeds = jax.random.split(jax.random.key(seed), 9)
    return {
        "sources": draw_sources(jax.random.fold_in(seeds[8], 71), 0),
        "targets": draw_targets(jax.random.fold_in(seeds[8], 71), 0),
        "target_lists": draw_target_lists(jax.random.fold_in(seeds[8], 71), 0),
        "target_clusters": place_ends(jax.random.randint(seeds[3], (NT,), 0, KC), jax.random.fold_in(seeds[3], 1), 0, KC - 1).astype(jnp.int32),
        "centroids_src": centred(seeds[4], (KC, D), 1.0, 6.0, ((0, 32),)),
        "centroids_tgt": centred(seeds[5], (KC, D), 1.0, 6.0, ((0, 8), (1, 4))),
        "sender_mean_measure": jnp.clip(jnp.exp(math.log(20.0) - 5.9914645 * jax.random.uniform(seeds[6], (KC,), jnp.float32) ** levels(seeds[6], (KC,), ((0, 4),), -0.2, 0.2)), 0.05, 20.0),
        "recipient_mean_measure": jnp.clip(jnp.exp(math.log(20.0) - 5.9914645 * jax.random.uniform(seeds[7], (KC,), jnp.float32) ** levels(seeds[7], (KC,), ((0, 8),), -0.2, 0.2)), 0.05, 20.0),
    }


heat_parameter = 0.02


def pair_cost(left_rows, right_rows):
    feature_count = left_rows.shape[1]
    left_sq = jnp.sum(jnp.square(left_rows.astype(jnp.float32)), axis=1)
    right_sq = jnp.sum(jnp.square(right_rows.astype(jnp.float32)), axis=1)
    cross_term = jnp.dot(left_rows, right_rows.T, preferred_element_type=jnp.float32)
    return (left_sq[:, None] + right_sq[None, :] - 2.0 * cross_term) / feature_count


def reference(sources, targets, target_lists, target_clusters, centroids_src, centroids_tgt, sender_mean_measure, recipient_mean_measure):
    feature_count = sources.shape[1]
    blurred_stratum = pair_cost(centroids_src, centroids_tgt)
    ln_sender_measure = heat_parameter * jnp.log(sender_mean_measure)
    ln_recipient_measure = heat_parameter * jnp.log(recipient_mean_measure)

    def coarse_turn(iteration, recipient_blurred_stratum):
        sender_blurred_stratum = ln_sender_measure - heat_parameter * jax.nn.logsumexp((recipient_blurred_stratum[None, :] - blurred_stratum) / heat_parameter, axis=1)
        return ln_recipient_measure - heat_parameter * jax.nn.logsumexp((sender_blurred_stratum[:, None] - blurred_stratum) / heat_parameter, axis=0)

    coarse_pot = lax.fori_loop(0, ITC, coarse_turn, jnp.zeros((KC,), jnp.float32))
    src_blocks = sources.reshape(NBLK, BLK, feature_count)
    tgt_blocks = targets.reshape(NBLK, BLK, feature_count)
    flat_lists = target_lists.reshape(-1)

    def entry_cost(block_pair):
        block_rows, block_list = block_pair
        listed = tgt_blocks[block_list]
        left_sq = jnp.sum(jnp.square(block_rows.astype(jnp.float32)), axis=1)
        right_sq = jnp.sum(jnp.square(listed.astype(jnp.float32)), axis=2)
        cross_term = jnp.einsum("id,lcd->lic", block_rows.astype(jnp.float32), listed.astype(jnp.float32))
        return (left_sq[None, :, None] + right_sq[:, None, :] - 2.0 * cross_term) / feature_count

    pointwise_charge = lax.map(entry_cost, (src_blocks, target_lists))
    recipient_kantorovich = coarse_pot[target_clusters].reshape(NBLK, BLK)

    def half_turn(block_pair):
        bandwise_charge, named_kantorovich = block_pair
        sender_figures = -heat_parameter * jax.nn.logsumexp((named_kantorovich[:, None, :] - bandwise_charge) / heat_parameter, axis=(0, 2))
        segment_lse_fold = jax.nn.logsumexp((sender_figures[None, :, None] - bandwise_charge) / heat_parameter, axis=1)
        return sender_figures, segment_lse_fold

    sender_kantorovich = jnp.zeros((NBLK, BLK), jnp.float32)
    for iteration in range(STEPS):
        sender_kantorovich, segment_lse_fold = lax.map(half_turn, (pointwise_charge, recipient_kantorovich[target_lists]))
        flat_part = segment_lse_fold.reshape(-1, BLK)
        best_rating = jnp.full((NBLK, BLK), -jnp.inf, jnp.float32).at[flat_lists].max(flat_part)
        ongoing_additions = jnp.zeros((NBLK, BLK), jnp.float32).at[flat_lists].add(jnp.exp(flat_part - best_rating[flat_lists]))
        recipient_kantorovich = -heat_parameter * (best_rating + jnp.log(ongoing_additions))
    listed_final = recipient_kantorovich[target_lists]

    def bary_turn(carry, block_items):
        numerators, denominators = carry
        block_rows, block_list, bandwise_charge, sender_band_members, named_kantorovich = block_items
        joint_measure_shares_entrywise = jnp.exp((sender_band_members[None, :, None] + named_kantorovich[:, None, :] - bandwise_charge) / heat_parameter).astype(jnp.bfloat16)
        weights_wide = lax.optimization_barrier(joint_measure_shares_entrywise).astype(jnp.float32)
        listed = tgt_blocks[block_list].astype(jnp.float32)
        src_num = jnp.einsum("lic,lcd->id", weights_wide, listed)
        src_den = jnp.sum(weights_wide, axis=(0, 2))
        src_mean = (src_num / src_den[:, None]).astype(jnp.bfloat16)
        tgt_part = jnp.einsum("lic,id->lcd", weights_wide, block_rows.astype(jnp.float32)).astype(jnp.bfloat16)
        tgt_part = lax.optimization_barrier(tgt_part).astype(jnp.float32)
        tgt_weight = jnp.sum(weights_wide, axis=1).astype(jnp.bfloat16)
        tgt_weight = lax.optimization_barrier(tgt_weight).astype(jnp.float32)
        return (numerators.at[block_list].add(tgt_part), denominators.at[block_list].add(tgt_weight)), src_mean

    initial = (jnp.zeros((NBLK, BLK, feature_count), jnp.float32), jnp.zeros((NBLK, BLK), jnp.float32))
    (numerators, denominators), src_means = lax.scan(bary_turn, initial, (src_blocks, target_lists, pointwise_charge, sender_kantorovich, listed_final))
    src_bary = src_means.reshape(NS, feature_count)
    tgt_bary = (numerators / denominators[:, :, None]).astype(jnp.bfloat16).reshape(NT, feature_count)
    return src_bary, tgt_bary, sender_kantorovich.reshape(NS), recipient_kantorovich.reshape(NT)
```

```python
import functools
import math

import jax
import jax.numpy as jnp
from jax import lax
from jax.experimental import pallas as pl
from jax.experimental.pallas import tpu as pltpu
from jax.sharding import PartitionSpec as P

BLK = 128
LIST = 4
ITC = 6
STEPS = 3
HEAT = 0.02
LOG2E = math.log2(math.e)
UNIT = LOG2E / HEAT
GROUP = 4
VMEM_LIMIT = 60 * 1024 * 1024
NEG = -jnp.inf
NT = (((1,), (1,)), ((), ()))


def to_narrow(index):
    return {"narrow": index}


def to_wide(index):
    return {"wide": index}


def remote(src, dst, send, recv, target):
    return pltpu.make_async_remote_copy(
        src_ref=src,
        dst_ref=dst,
        send_sem=send,
        recv_sem=recv,
        device_id=target,
        device_id_type=pl.DeviceIdType.MESH,
    )


def barrier(n, w):
    me_n = lax.axis_index("narrow")
    me_w = lax.axis_index("wide")
    sem = pltpu.get_barrier_semaphore()
    for p in range(1, n):
        pl.semaphore_signal(
            sem, inc=1, device_id=to_narrow(lax.rem(me_n + p, n)), device_id_type=pl.DeviceIdType.MESH
        )
    for p in range(1, w):
        pl.semaphore_signal(
            sem, inc=1, device_id=to_wide(lax.rem(me_w + p, w)), device_id_type=pl.DeviceIdType.MESH
        )
    pl.semaphore_wait(sem, n - 1 + w - 1)


class Gather:
    def __init__(self, n, src, slot, send, recv):
        self.n, self.half = n, n // 2
        self.me = lax.axis_index("narrow")
        self.partner = self.me + 1 - 2 * lax.rem(self.me, 2)
        self.src, self.slot, self.send, self.recv = src, slot, send, recv

    def direct(self, p):
        return remote(
            self.src,
            self.slot(self.me),
            self.send(p - 1),
            self.recv(p - 1),
            to_narrow(lax.rem(self.me + 2 * p, self.n)),
        )

    def landed(self, p):
        at = self.slot(lax.rem(self.me + self.n - 2 * p, self.n))
        return remote(
            at, at, self.send(p - 1), self.recv(p - 1), to_narrow(lax.rem(self.me + 2 * p, self.n))
        )

    def own_pair(self):
        j = self.half - 1
        return remote(self.src, self.slot(self.me), self.send(j), self.recv(j), to_narrow(self.partner))

    def passed(self, p):
        j = self.half - 1 + p
        at = self.slot(lax.rem(self.me + self.n - 2 * p, self.n))
        return remote(at, at, self.send(j), self.recv(j), to_narrow(self.partner))

    def start(self):
        for p in range(1, self.half):
            self.direct(p).start()
        self.own_pair().start()

    def forward(self):
        for p in range(1, self.half):
            self.landed(p).wait_recv()
            self.passed(p).start()

    def finish(self):
        j = self.half - 1
        at = self.slot(self.partner)
        remote(at, at, self.send(j), self.recv(j), to_narrow(self.partner)).wait_recv()
        for p in range(1, self.half):
            j = self.half - 1 + p
            at = self.slot(lax.rem(self.partner + self.n - 2 * p, self.n))
            remote(at, at, self.send(j), self.recv(j), to_narrow(self.partner)).wait_recv()
        for p in range(1, self.half):
            self.direct(p).wait_send()
        self.own_pair().wait_send()
        for p in range(1, self.half):
            self.passed(p).wait_send()


def diagonal():
    return lax.broadcasted_iota(jnp.int32, (BLK, BLK), 0) == lax.broadcasted_iota(
        jnp.int32, (BLK, BLK), 1
    )


def as_row(column, diag):
    return jnp.sum(jnp.where(diag, column, 0.0), axis=0, keepdims=True)


def coarse_kernel(
    n,
    w,
    cs_ref,
    ct_ref,
    mu_ref,
    nu_ref,
    x_ref,
    y_ref,
    pot_ref,
    xall_ref,
    yall_ref,
    frag,
    panel,
    tile,
    frep,
    frow,
    gcol,
    bsq,
    row_out,
    row_in,
    col_out,
    col_in,
    last_in,
    fs,
    fr,
    ps,
    pr,
    bs,
    br,
    rs,
    rr,
    ks,
    kr,
    ls,
    lr,
    loc,
):
    me_n = lax.axis_index("narrow")
    me_w = lax.axis_index("wide")
    rb = cs_ref.shape[1]
    cols = ct_ref.shape[0]
    rows = rb * n
    groups = rows // BLK
    features = ct_ref.shape[1] * w
    own_rows = x_ref.shape[0]
    chunks = ITC + 2
    step_rows = own_rows // chunks
    barrier(n, w)
    diag = diagonal()

    local = [
        pltpu.make_async_copy(cs_ref, frag.at[me_n], loc.at[0]),
        pltpu.make_async_copy(ct_ref, panel.at[me_w], loc.at[1]),
        pltpu.make_async_copy(y_ref, yall_ref.at[me_n], loc.at[2]),
        pltpu.make_async_copy(x_ref, xall_ref.at[me_n], loc.at[3]),
    ]
    fg = Gather(n, cs_ref, lambda i: frag.at[i], lambda j: fs.at[j], lambda j: fr.at[j])
    fg.start()
    panels = []
    for p in range(1, w):
        c = remote(ct_ref, panel.at[me_w], ps.at[p - 1], pr.at[p - 1], to_wide(lax.rem(me_w + p, w)))
        c.start()
        panels.append(c)
    for c in local:
        c.start()

    def bulk(which, c):
        src, dst = ((y_ref, yall_ref), (x_ref, xall_ref))[which]
        at = pl.ds(pl.multiple_of(c * step_rows, step_rows), step_rows)
        return Gather(
            n,
            src.at[at],
            lambda i: dst.at[i, at],
            lambda j: bs.at[which, c, j],
            lambda j: br.at[which, c, j],
        )

    fg.forward()
    for c in range(2):
        bulk(0, c).start()
        bulk(1, c).start()
    fg.finish()
    for p in range(1, w):
        at = panel.at[lax.rem(me_w + w - p, w)]
        remote(at, at, ps.at[p - 1], pr.at[p - 1], to_wide(lax.rem(me_w + p, w))).wait_recv()
    for c in panels:
        c.wait_send()
    local[0].wait()
    local[1].wait()

    unit = 2.0 * UNIT / features
    half = min(cols, 512)

    def product(i, carry):
        for c in range(cols // half):
            acc = None
            for k in range(w):
                d = lax.dot_general(
                    frag[i, k], panel[k, c * half : (c + 1) * half, :], NT, preferred_element_type=jnp.float32
                )
                acc = d if acc is None else acc + d
            tile[pl.ds(pl.multiple_of(i * rb, rb), rb), c * half : (c + 1) * half] = acc * unit
        return carry

    lax.fori_loop(0, n, product, 0)
    for g in range(cols // BLK):
        sq = jnp.zeros((BLK, 1), jnp.float32)
        for k in range(w):
            v = panel[k, g * BLK : (g + 1) * BLK, :].astype(jnp.float32)
            sq = sq + jnp.sum(v * v, axis=1, keepdims=True)
        bsq[:, g * BLK : (g + 1) * BLK] = as_row(sq, diag) * (UNIT / features)
    gcol[...] = -bsq[...]
    sub = 32
    cg = cols // BLK

    def turn(it, carry):
        g_now = gcol[...]

        def row_group(g, c2):
            ms, zs = [], []
            for s in range(BLK // sub):
                start = pl.multiple_of(g * BLK + s * sub, sub)
                t = tile[pl.ds(start, sub), :] + g_now
                m = jnp.max(t, axis=1, keepdims=True)
                z = jnp.sum(jnp.exp2(t - m), axis=1, keepdims=True)
                ms.append(m)
                zs.append(z)
            row_out[it, pl.ds(g, 1), :] = as_row(jnp.concatenate(ms, axis=0), diag)
            row_out[it, pl.ds(groups + g, 1), :] = as_row(jnp.concatenate(zs, axis=0), diag)
            return c2

        lax.fori_loop(0, groups, row_group, 0)
        sent = []
        for p in range(1, n):
            c = remote(
                row_out.at[it],
                row_in.at[it, p - 1],
                rs.at[it, p - 1],
                rr.at[it, p - 1],
                to_narrow(lax.rem(me_n + p, n)),
            )
            c.start()
            sent.append(c)
        bulk(0, it + 2).start()
        for c in sent:
            c.wait_recv()
        top = row_out[it, 0:groups, :]
        for p in range(n - 1):
            top = jnp.maximum(top, row_in[it, p, 0:groups, :])
        total = row_out[it, groups : 2 * groups, :] * jnp.exp2(row_out[it, 0:groups, :] - top)
        for p in range(n - 1):
            total = total + row_in[it, p, groups : 2 * groups, :] * jnp.exp2(
                row_in[it, p, 0:groups, :] - top
            )
        frow[...] = jnp.log2(mu_ref[...]) - (top + jnp.log2(total))
        bulk(0, it).forward()

        def spread(g, c2):
            line = jnp.broadcast_to(frow[pl.ds(g, 1), :], (BLK, BLK))
            frep[pl.ds(pl.multiple_of(g * BLK, BLK), BLK), :] = line.T
            return c2

        lax.fori_loop(0, groups, spread, 0)
        span = 64

        def top_step(r, tops):
            start = pl.multiple_of(r * span, span)
            f = frep[pl.ds(start, span), :]
            out = []
            for c in range(cg):
                t = f + tile[pl.ds(start, span), c * BLK : (c + 1) * BLK]
                out.append(jnp.maximum(tops[c], jnp.max(t.reshape(span // 8, 8, BLK), axis=0)))
            return tuple(out)

        tops = lax.fori_loop(
            0, rows // span, top_step, tuple(jnp.full((8, BLK), NEG, jnp.float32) for _ in range(cg))
        )
        tops = tuple(jnp.broadcast_to(jnp.max(t, axis=0, keepdims=True), (8, BLK)) for t in tops)

        def sum_step(r, sums):
            start = pl.multiple_of(r * span, span)
            f = frep[pl.ds(start, span), :]
            out = []
            for c in range(cg):
                t = (f + tile[pl.ds(start, span), c * BLK : (c + 1) * BLK]).reshape(span // 8, 8, BLK)
                out.append(sums[c] + jnp.sum(jnp.exp2(t - tops[c][None]), axis=0))
            return tuple(out)

        sums = lax.fori_loop(
            0, rows // span, sum_step, tuple(jnp.zeros((8, BLK), jnp.float32) for _ in range(cg))
        )
        for c in range(cg):
            col_out[it, 0:1, c * BLK : (c + 1) * BLK] = tops[c][0:1]
            col_out[it, 1:2, c * BLK : (c + 1) * BLK] = jnp.sum(sums[c], axis=0, keepdims=True)
        csent = []
        for p in range(1, w):
            c = remote(
                col_out.at[it],
                col_in.at[it, p - 1],
                ks.at[it, p - 1],
                kr.at[it, p - 1],
                to_wide(lax.rem(me_w + p, w)),
            )
            c.start()
            csent.append(c)
        bulk(1, it + 2).start()
        for c in csent:
            c.wait_recv()
        top = col_out[it, 0:1, :]
        for p in range(w - 1):
            top = jnp.maximum(top, col_in[it, p, 0:1, :])
        total = col_out[it, 1:2, :] * jnp.exp2(col_out[it, 0:1, :] - top)
        for p in range(w - 1):
            total = total + col_in[it, p, 1:2, :] * jnp.exp2(col_in[it, p, 0:1, :] - top)
        gcol[...] = jnp.log2(nu_ref[...]) - (top + jnp.log2(total))
        bulk(1, it).forward()
        for c in sent:
            c.wait_send()
        for c in csent:
            c.wait_send()
        return carry

    lax.fori_loop(0, ITC, turn, 0)
    gcol[...] = gcol[...] + bsq[...]
    last = []
    for p in range(1, n):
        c = remote(
            gcol, last_in.at[p - 1], ls.at[p - 1], lr.at[p - 1], to_narrow(lax.rem(me_n + p, n))
        )
        c.start()
        last.append(c)
    pot_ref[me_n] = gcol[...]
    for c in last:
        c.wait_recv()
    for p in range(1, n):
        pot_ref[lax.rem(me_n + n - p, n)] = last_in[p - 1]
    for c in last:
        c.wait_send()
    for c in range(ITC, chunks):
        bulk(0, c).forward()
        bulk(1, c).forward()

    def close(c, carry):
        bulk(0, c).finish()
        bulk(1, c).finish()
        return carry

    lax.fori_loop(0, chunks, close, 0)
    local[2].wait()
    local[3].wait()


def coarse_call(n, w, cs, ct, mu, nu, x, y):
    rb = cs.shape[1]
    cols, part = ct.shape
    rows = rb * n
    groups = rows // BLK
    chunks = ITC + 2
    dma = pltpu.SemaphoreType.DMA
    vm = pl.BlockSpec(memory_space=pltpu.VMEM)
    anyspace = pl.BlockSpec(memory_space=pl.ANY)
    f32 = jnp.float32
    return pl.pallas_call(
        functools.partial(coarse_kernel, n, w),
        out_shape=(
            jax.ShapeDtypeStruct((n, 1, cols), f32),
            jax.ShapeDtypeStruct((n,) + x.shape, x.dtype),
            jax.ShapeDtypeStruct((n,) + y.shape, y.dtype),
        ),
        in_specs=[vm] * 6,
        out_specs=(vm, anyspace, anyspace),
        scratch_shapes=[
            pltpu.VMEM((n, w, rb, part), cs.dtype),
            pltpu.VMEM((w, cols, part), ct.dtype),
            pltpu.VMEM((rows, cols), f32),
            pltpu.VMEM((rows, BLK), f32),
            pltpu.VMEM((groups, BLK), f32),
            pltpu.VMEM((1, cols), f32),
            pltpu.VMEM((1, cols), f32),
            pltpu.VMEM((ITC, 2 * groups, BLK), f32),
            pltpu.VMEM((ITC, n - 1, 2 * groups, BLK), f32),
            pltpu.VMEM((ITC, 2, cols), f32),
            pltpu.VMEM((ITC, w - 1, 2, cols), f32),
            pltpu.VMEM((n - 1, 1, cols), f32),
            dma((n - 1,)),
            dma((n - 1,)),
            dma((w - 1,)),
            dma((w - 1,)),
            dma((2, chunks, n - 1)),
            dma((2, chunks, n - 1)),
            dma((ITC, n - 1)),
            dma((ITC, n - 1)),
            dma((ITC, w - 1)),
            dma((ITC, w - 1)),
            dma((n - 1,)),
            dma((n - 1,)),
            dma((4,)),
        ],
        compiler_params=pltpu.CompilerParams(
            collective_id=0, has_side_effects=True, vmem_limit_bytes=VMEM_LIMIT
        ),
        name="coarse",
    )(cs, ct, mu, nu, x, y)


def score_kernel(unit, row_pick, index_ref, own_ref, *refs):
    out = refs[-1]
    step = pl.program_id(0)
    for l in range(GROUP):
        left = own_ref[row_pick(index_ref, step, l)]
        out[l] = lax.dot_general(left, refs[l][0], NT, preferred_element_type=jnp.float32) * unit


def score_call(unit, row_pick, meta, own, pool, entries):
    feature_count = own.shape[-1]

    def pick(l):
        return lambda i, meta_ref: (meta_ref[0, i * GROUP + l], 0, 0)

    return pl.pallas_call(
        functools.partial(score_kernel, unit, row_pick),
        out_shape=jax.ShapeDtypeStruct((entries, BLK, BLK), jnp.float32),
        grid_spec=pltpu.PrefetchScalarGridSpec(
            num_scalar_prefetch=1,
            grid=(entries // GROUP,),
            in_specs=[pl.BlockSpec(own.shape, lambda i, m: (0, 0, 0))]
            + [pl.BlockSpec((1, BLK, feature_count), pick(l)) for l in range(GROUP)],
            out_specs=pl.BlockSpec((GROUP, BLK, BLK), lambda i, m: (i, 0, 0)),
        ),
        compiler_params=pltpu.CompilerParams(vmem_limit_bytes=VMEM_LIMIT),
        name="scores",
    )(meta, own, *([pool] * GROUP))


def fine_kernel(
    n,
    w,
    smeta,
    tmeta,
    ms_ref,
    mt_ref,
    live_ref,
    coarse_ref,
    cl_ref,
    asq_ref,
    bsq_ref,
    fpot_ref,
    gpot_ref,
    ps_ref,
    pt_ref,
    *scratch,
):
    pots = scratch[: 2 * STEPS + 1]
    own_g, mbuf, zbuf, send, recv = scratch[2 * STEPS + 1 :]
    me_n = lax.axis_index("narrow")
    sb = asq_ref.shape[0]
    tb = bsq_ref.shape[0]
    slots = mt_ref.shape[0]
    barrier(n, w)
    diag = diagonal()

    def region(i, count):
        return pl.ds(pl.multiple_of(i * count, count), count)

    def share(x, count):
        for p in range(1, n):
            at = pots[x].at[region(me_n, count)]
            remote(
                at, at, send.at[x, p - 1], recv.at[x, p - 1], to_narrow(lax.rem(me_n + p, n))
            ).start()

    def arrive(x, count):
        for p in range(1, n):
            at = pots[x].at[region(lax.rem(me_n + n - p, n), count)]
            remote(
                at, at, send.at[x, p - 1], recv.at[x, p - 1], to_narrow(lax.rem(me_n + p, n))
            ).wait_recv()
        for p in range(1, n):
            at = pots[x].at[region(me_n, count)]
            remote(
                at, at, send.at[x, p - 1], recv.at[x, p - 1], to_narrow(lax.rem(me_n + p, n))
            ).wait_send()

    points = cl_ref.shape[1]
    hi = coarse_ref.shape[1]
    clusters = cl_ref[...]
    spread = jnp.where(
        lax.broadcasted_iota(jnp.int32, (hi, points), 0) == clusters // BLK, 1.0, 0.0
    ).astype(jnp.float32)
    picked = jnp.dot(
        coarse_ref[...], spread, preferred_element_type=jnp.float32, precision=lax.Precision.HIGHEST
    )
    lane = lax.broadcasted_iota(jnp.int32, (BLK, points), 0) == lax.rem(clusters, BLK)
    begin = jnp.sum(jnp.where(lane, picked, 0.0), axis=0, keepdims=True)
    for b in range(tb):
        pots[0][pl.ds(me_n * tb + b, 1), :] = (
            begin[:, b * BLK : (b + 1) * BLK] - bsq_ref[b : b + 1, :]
        )
    share(0, tb)

    for k in range(STEPS):
        gx = 2 * k
        fx = 2 * k + 1
        nx = 2 * k + 2
        arrive(gx, tb)

        def src_block(b, c2, gx=gx, fx=fx):
            ts = []
            top = None
            for l in range(LIST):
                e = b * LIST + l
                t = ms_ref[e] + pots[gx][pl.ds(smeta[e], 1), :]
                ts.append(t)
                top = t if top is None else jnp.maximum(top, t)
            top = jnp.max(top, axis=1, keepdims=True)
            total = None
            for t in ts:
                v = jnp.exp2(t - top)
                total = v if total is None else total + v
            total = jnp.sum(total, axis=1, keepdims=True)
            pots[fx][pl.ds(me_n * sb + b, 1), :] = as_row(-(top + jnp.log2(total)), diag)
            return c2

        lax.fori_loop(0, sb, src_block, 0)
        share(fx, sb)
        arrive(fx, sb)

        def slot_step(s, c2, fx=fx):
            for u in range(2):
                e = s * 2 + u
                t = mt_ref[e] + pots[fx][pl.ds(tmeta[0, e], 1), :]
                top = jnp.max(t, axis=1, keepdims=True)
                total = jnp.sum(jnp.exp2(t - top), axis=1, keepdims=True)
                mbuf[pl.ds(e, 1), :] = as_row(top, diag)
                zbuf[pl.ds(e, 1), :] = as_row(total, diag)
            return c2

        lax.fori_loop(0, slots // 2, slot_step, 0)
        live = live_ref[...]
        m_all = mbuf[...]
        z_all = zbuf[...]
        for b in range(tb):
            mask = live == b
            top = jnp.max(jnp.where(mask, m_all, NEG), axis=0, keepdims=True)
            part = z_all * jnp.exp2(jnp.where(mask, m_all - top, 0.0))
            total = jnp.sum(jnp.where(mask, part, 0.0), axis=0, keepdims=True)
            line = -(top + jnp.log2(total))
            pots[nx][pl.ds(me_n * tb + b, 1), :] = line
            own_g[b : b + 1, :] = line
        share(nx, tb)

    fx, gx = 2 * STEPS - 1, 2 * STEPS

    def target_plan(s, c2):
        g_line = own_g[pl.ds(tmeta[1, s], 1), :]
        g_col = jnp.broadcast_to(g_line, (BLK, BLK)).T
        t = mt_ref[s] + pots[fx][pl.ds(tmeta[0, s], 1), :] + g_col
        alive = live_ref[pl.ds(s, 1), :] >= 0
        pt_ref[s] = jnp.where(alive, jnp.exp2(t), 0.0).astype(jnp.bfloat16)
        return c2

    lax.fori_loop(0, slots, target_plan, 0)
    fpot_ref[...] = (pots[fx][region(me_n, sb), :] + asq_ref[...]) * (1.0 / UNIT)
    gpot_ref[...] = (own_g[...] + bsq_ref[...]) * (1.0 / UNIT)
    arrive(gx, tb)

    def source_plan(b, c2):
        f_line = pots[fx][pl.ds(me_n * sb + b, 1), :]
        f_col = jnp.broadcast_to(f_line, (BLK, BLK)).T
        for l in range(LIST):
            e = b * LIST + l
            t = ms_ref[e] + pots[gx][pl.ds(smeta[e], 1), :] + f_col
            ps_ref[e] = jnp.exp2(t).astype(jnp.bfloat16)
        return c2

    lax.fori_loop(0, sb, source_plan, 0)


def fine_call(n, w, smeta, tmeta, ms, mt, live, coarse, clusters, asq, bsq):
    vm = pl.BlockSpec(memory_space=pltpu.VMEM)
    sm = pl.BlockSpec(memory_space=pltpu.SMEM)
    dma = pltpu.SemaphoreType.DMA
    f32 = jnp.float32
    turns = 2 * STEPS + 1
    held = n * max(asq.shape[0], bsq.shape[0])
    slots = mt.shape[0]
    return pl.pallas_call(
        functools.partial(fine_kernel, n, w),
        out_shape=(
            jax.ShapeDtypeStruct(asq.shape, f32),
            jax.ShapeDtypeStruct(bsq.shape, f32),
            jax.ShapeDtypeStruct(ms.shape, jnp.bfloat16),
            jax.ShapeDtypeStruct(mt.shape, jnp.bfloat16),
        ),
        in_specs=[sm, sm] + [vm] * 7,
        out_specs=(vm,) * 4,
        scratch_shapes=[
            *[pltpu.VMEM((held, BLK), f32) for _ in range(turns)],
            pltpu.VMEM(bsq.shape, f32),
            pltpu.VMEM((slots, BLK), f32),
            pltpu.VMEM((slots, BLK), f32),
            dma((turns, n - 1)),
            dma((turns, n - 1)),
        ],
        compiler_params=pltpu.CompilerParams(
            collective_id=1, has_side_effects=True, vmem_limit_bytes=VMEM_LIMIT
        ),
        name="fine",
    )(smeta, tmeta, ms, mt, live, coarse, clusters, asq, bsq)


def source_mean_kernel(meta, plan_ref, *refs):
    out = refs[-1]
    num = None
    den = None
    for l in range(LIST):
        p = plan_ref[l]
        d = jnp.dot(p, refs[l][0], preferred_element_type=jnp.float32)
        s = p.astype(jnp.float32)
        num = d if num is None else num + d
        den = s if den is None else den + s
    out[...] = (num / jnp.sum(den, axis=1, keepdims=True)).astype(out.dtype)


def source_mean(meta, plan, pool):
    entries = plan.shape[0]
    feature_count = pool.shape[-1]

    def pick(l):
        return lambda i, m: (m[0, i * LIST + l], 0, 0)

    return pl.pallas_call(
        source_mean_kernel,
        out_shape=jax.ShapeDtypeStruct((entries // LIST * BLK, feature_count), pool.dtype),
        grid_spec=pltpu.PrefetchScalarGridSpec(
            num_scalar_prefetch=1,
            grid=(entries // LIST,),
            in_specs=[pl.BlockSpec((LIST, BLK, BLK), lambda i, m: (i, 0, 0))]
            + [pl.BlockSpec((1, BLK, feature_count), pick(l)) for l in range(LIST)],
            out_specs=pl.BlockSpec((BLK, feature_count), lambda i, m: (i, 0)),
        ),
        compiler_params=pltpu.CompilerParams(vmem_limit_bytes=VMEM_LIMIT),
        name="source_mean",
    )(meta, plan, *([pool] * LIST))


def target_mean_kernel(tb, meta, plan_ref, *refs):
    blocks, (out, num, den) = refs[:GROUP], refs[GROUP:]
    step = pl.program_id(0)

    @pl.when(step == 0)
    def _():
        num[...] = jnp.zeros_like(num)
        den[...] = jnp.zeros_like(den)

    for l in range(GROUP):
        t = meta[1, step * GROUP + l]
        p = plan_ref[l]
        num[t] += jnp.dot(p, blocks[l][0], preferred_element_type=jnp.float32)
        den[t] += p.astype(jnp.float32)

    @pl.when(step == pl.num_programs(0) - 1)
    def _():
        def write(t, carry):
            total = jnp.sum(den[t], axis=1, keepdims=True)
            out[pl.ds(pl.multiple_of(t * BLK, BLK), BLK), :] = (num[t] / total).astype(out.dtype)
            return carry

        lax.fori_loop(0, tb, write, 0)


def target_mean(tb, meta, plan, pool):
    slots = plan.shape[0]
    feature_count = pool.shape[-1]

    def pick(l):
        return lambda i, m: (m[0, i * GROUP + l], 0, 0)

    return pl.pallas_call(
        functools.partial(target_mean_kernel, tb),
        out_shape=jax.ShapeDtypeStruct((tb * BLK, feature_count), pool.dtype),
        grid_spec=pltpu.PrefetchScalarGridSpec(
            num_scalar_prefetch=1,
            grid=(slots // GROUP,),
            in_specs=[pl.BlockSpec((GROUP, BLK, BLK), lambda i, m: (i, 0, 0))]
            + [pl.BlockSpec((1, BLK, feature_count), pick(l)) for l in range(GROUP)],
            out_specs=pl.BlockSpec((tb * BLK, feature_count), lambda i, m: (0, 0)),
            scratch_shapes=[
                pltpu.VMEM((tb, BLK, feature_count), jnp.float32),
                pltpu.VMEM((tb, BLK, BLK), jnp.float32),
            ],
        ),
        compiler_params=pltpu.CompilerParams(vmem_limit_bytes=VMEM_LIMIT),
        name="target_mean",
    )(meta, plan, *([pool] * GROUP))


def square_norms(rows_in):
    return jnp.sum(jnp.square(rows_in.astype(jnp.float32)), axis=-1)


def own_block_of_entry(meta_ref, step, l):
    return step


def own_block_of_slot(meta_ref, step, l):
    return meta_ref[1, step * GROUP + l]


def body(
    sources,
    targets,
    target_lists,
    target_clusters,
    centroids_src,
    centroids_tgt,
    sender_mean_measure,
    recipient_mean_measure,
):
    feature_count = sources.shape[1]
    n = lax.axis_size("narrow")
    w = lax.axis_size("wide")
    sb = sources.shape[0] // BLK
    tb = targets.shape[0] // BLK
    wanted = target_lists.reshape(-1)
    entries = wanted.shape[0]
    capacity = max(
        (5 * sb * LIST + 4 * n - 1) // (4 * n),
        (tb + n - 1) // n,
    )
    slots = n * capacity
    index = jnp.arange(entries, dtype=jnp.int32)
    owner_of = wanted // tb % n
    local_block = wanted % tb
    earlier = jnp.logical_and(owner_of[:, None] == owner_of[None, :], index[None, :] < index[:, None])
    slot_of = owner_of * capacity + jnp.sum(earlier.astype(jnp.int32), axis=1)
    code = local_block + tb * (index // LIST) + 1
    hit = slot_of[None, :] == jnp.arange(slots, dtype=jnp.int32)[:, None]
    requests = jnp.sum(jnp.where(hit, code[None, :], 0), axis=1).reshape(n, capacity)
    asked = lax.all_to_all(requests, "narrow", split_axis=0, concat_axis=0, tiled=True)
    asked = asked.reshape(-1) - 1
    alive = asked >= 0
    clipped = jnp.maximum(asked, 0)
    from_block = (jnp.arange(slots, dtype=jnp.int32) // capacity) * sb + clipped // tb
    to_block = clipped % tb
    tmeta = jnp.stack([from_block, to_block])
    live = jnp.broadcast_to(jnp.where(alive, to_block, -1)[:, None], (slots, BLK))
    smeta = owner_of * tb + local_block

    cs = centroids_src.reshape(centroids_src.shape[0], w, -1).transpose(1, 0, 2)
    mu = sender_mean_measure.reshape(-1, BLK)
    nu = recipient_mean_measure.reshape(1, -1)
    coarse, xall, yall = coarse_call(n, w, cs, centroids_tgt, mu, nu, sources, targets)
    xall = xall.reshape(n * sb, BLK, feature_count)
    yall = yall.reshape(n * tb, BLK, feature_count)
    src_blocks = sources.reshape(sb, BLK, feature_count)
    tgt_blocks = targets.reshape(tb, BLK, feature_count)
    unit = 2.0 * UNIT / feature_count
    ms = score_call(unit, own_block_of_entry, smeta[None, :], src_blocks, yall, entries)
    mt = score_call(unit, own_block_of_slot, tmeta, tgt_blocks, xall, slots)
    asq = square_norms(src_blocks) * (UNIT / feature_count)
    bsq = square_norms(tgt_blocks) * (UNIT / feature_count)
    src_potential, tgt_potential, ps, pt = fine_call(
        n,
        w,
        smeta,
        tmeta,
        ms,
        mt,
        live,
        coarse.reshape(-1, BLK).T,
        target_clusters.reshape(1, -1),
        asq,
        bsq,
    )
    src_bary = source_mean(smeta[None, :], ps, yall)
    tgt_bary = target_mean(tb, tmeta, pt, xall)
    return (src_bary, tgt_bary, src_potential.reshape(-1), tgt_potential.reshape(-1))


def solution(mesh):
    in_specs = (
        P(("wide", "narrow"), None),
        P(("wide", "narrow"), None),
        P(("wide", "narrow"), None),
        P(("wide", "narrow")),
        P(("wide", "narrow"), None),
        P("narrow", "wide"),
        P("wide"),
        P("narrow"),
    )
    out_specs = (
        P(("wide", "narrow"), None),
        P(("wide", "narrow"), None),
        P(("wide", "narrow")),
        P(("wide", "narrow")),
    )
    return jax.shard_map(body, mesh=mesh, in_specs=in_specs, out_specs=out_specs, check_vma=False)
```

```python
import functools
import math

import jax
import jax.numpy as jnp
from jax import lax
from jax.experimental import pallas as pl
from jax.experimental.pallas import tpu as pltpu
from jax.sharding import PartitionSpec as P

BLK = 128
LIST = 4
ITC = 6
STEPS = 3
HEAT = 0.02
LOG2E = math.log2(math.e)
UNIT = LOG2E / HEAT
GROUP = 4
VMEM_LIMIT = 60 * 1024 * 1024
NEG = -jnp.inf
NT = (((1,), (1,)), ((), ()))


def to_narrow(index):
    return {"narrow": index}


def to_wide(index):
    return {"wide": index}


def remote(src, dst, send, recv, target):
    return pltpu.make_async_remote_copy(
        src_ref=src,
        dst_ref=dst,
        send_sem=send,
        recv_sem=recv,
        device_id=target,
        device_id_type=pl.DeviceIdType.MESH,
    )


def barrier(n, w):
    me_n = lax.axis_index("narrow")
    me_w = lax.axis_index("wide")
    sem = pltpu.get_barrier_semaphore()
    for p in range(1, n):
        pl.semaphore_signal(
            sem, inc=1, device_id=to_narrow(lax.rem(me_n + p, n)), device_id_type=pl.DeviceIdType.MESH
        )
    for p in range(1, w):
        pl.semaphore_signal(
            sem, inc=1, device_id=to_wide(lax.rem(me_w + p, w)), device_id_type=pl.DeviceIdType.MESH
        )
    pl.semaphore_wait(sem, n - 1 + w - 1)


class Gather:
    def __init__(self, n, src, slot, send, recv):
        self.n, self.half = n, n // 2
        self.me = lax.axis_index("narrow")
        self.partner = self.me + 1 - 2 * lax.rem(self.me, 2)
        self.src, self.slot, self.send, self.recv = src, slot, send, recv

    def direct(self, p):
        return remote(
            self.src,
            self.slot(self.me),
            self.send(p - 1),
            self.recv(p - 1),
            to_narrow(lax.rem(self.me + 2 * p, self.n)),
        )

    def landed(self, p):
        at = self.slot(lax.rem(self.me + self.n - 2 * p, self.n))
        return remote(
            at, at, self.send(p - 1), self.recv(p - 1), to_narrow(lax.rem(self.me + 2 * p, self.n))
        )

    def own_pair(self):
        j = self.half - 1
        return remote(self.src, self.slot(self.me), self.send(j), self.recv(j), to_narrow(self.partner))

    def passed(self, p):
        j = self.half - 1 + p
        at = self.slot(lax.rem(self.me + self.n - 2 * p, self.n))
        return remote(at, at, self.send(j), self.recv(j), to_narrow(self.partner))

    def start(self):
        for p in range(1, self.half):
            self.direct(p).start()
        self.own_pair().start()

    def forward(self):
        for p in range(1, self.half):
            self.landed(p).wait_recv()
            self.passed(p).start()

    def forward_far(self):
        pass

    def finish(self):
        j = self.half - 1
        at = self.slot(self.partner)
        remote(at, at, self.send(j), self.recv(j), to_narrow(self.partner)).wait_recv()
        for p in range(1, self.half):
            j = self.half - 1 + p
            at = self.slot(lax.rem(self.partner + self.n - 2 * p, self.n))
            remote(at, at, self.send(j), self.recv(j), to_narrow(self.partner)).wait_recv()
        for p in range(1, self.half):
            self.direct(p).wait_send()
        self.own_pair().wait_send()
        for p in range(1, self.half):
            self.passed(p).wait_send()


def flip(index, size):
    return index + size - 2 * size * lax.rem(index // size, 2)


class Relay:
    def __init__(self, src, slot, rows, send, recv):
        me = lax.axis_index("narrow")
        self.me, self.sib, self.xn, self.yn = me, flip(me, 1), flip(me, 2), flip(me, 4)
        self.far = flip(self.xn, 4)
        self.src, self.slot, self.send, self.recv = src, slot, send, recv
        self.low, self.high, self.full = pl.ds(0, rows // 2), pl.ds(rows // 2, rows // 2), pl.ds(0, rows)
        self.rows = rows

    def copy(self, j, src, dst, target):
        return remote(src, dst, self.send(j), self.recv(j), to_narrow(target))

    def through(self, j, owner, part, target):
        at = self.slot(owner, part)
        return self.copy(j, at, at, target)

    def own(self):
        at = self.slot(self.me, 0)
        return [self.copy(j, self.src, at, t) for j, t in enumerate((self.xn, self.yn, self.sib))]

    def relays(self):
        return [
            self.through(3, self.xn, 1, self.yn),
            self.through(4, self.yn, 2, self.xn),
            self.through(5, self.xn, 0, self.sib),
            self.through(6, self.yn, 0, self.sib),
        ]

    def corner(self):
        return self.through(7, self.far, 0, self.sib)

    def start(self):
        for c in self.own():
            c.start()

    def forward(self):
        self.through(0, self.xn, 0, self.xn).wait_recv()
        self.through(1, self.yn, 0, self.yn).wait_recv()
        for c in self.relays():
            c.start()

    def forward_far(self):
        self.through(3, self.far, 1, self.yn).wait_recv()
        self.through(4, self.far, 2, self.xn).wait_recv()
        self.corner().start()

    def finish(self):
        self.through(2, self.sib, 0, self.sib).wait_recv()
        self.through(5, flip(self.sib, 2), 0, self.sib).wait_recv()
        self.through(6, flip(self.sib, 4), 0, self.sib).wait_recv()
        self.through(7, flip(self.far, 1), 0, self.sib).wait_recv()
        for c in self.own() + self.relays() + [self.corner()]:
            c.wait_send()


def diagonal():
    return lax.broadcasted_iota(jnp.int32, (BLK, BLK), 0) == lax.broadcasted_iota(
        jnp.int32, (BLK, BLK), 1
    )


def as_row(column, diag):
    return jnp.sum(jnp.where(diag, column, 0.0), axis=0, keepdims=True)


def coarse_kernel(
    n,
    w,
    cs_ref,
    ct_ref,
    mu_ref,
    nu_ref,
    x_ref,
    y_ref,
    ask_ref,
    pot_ref,
    got_ref,
    xall_ref,
    yall_ref,
    frag,
    panel,
    tile,
    frep,
    frow,
    gcol,
    bsq,
    row_out,
    row_in,
    col_out,
    col_in,
    last_in,
    fs,
    fr,
    ps,
    pr,
    bs,
    br,
    rs,
    rr,
    ks,
    kr,
    ls,
    lr,
    qs,
    qr,
    loc,
):
    me_n = lax.axis_index("narrow")
    me_w = lax.axis_index("wide")
    rb = cs_ref.shape[1]
    cols = ct_ref.shape[0]
    rows = rb * n
    groups = rows // BLK
    features = ct_ref.shape[1] * w
    own_rows = x_ref.shape[0]
    chunks = ITC + 2
    step_rows = own_rows // chunks
    barrier(n, w)
    diag = diagonal()

    local = [
        pltpu.make_async_copy(cs_ref, frag.at[me_n], loc.at[0]),
        pltpu.make_async_copy(ct_ref, panel.at[me_w], loc.at[1]),
        pltpu.make_async_copy(y_ref, yall_ref.at[me_n], loc.at[2]),
        pltpu.make_async_copy(x_ref, xall_ref.at[me_n], loc.at[3]),
    ]
    fg = Gather(n, cs_ref, lambda i: frag.at[i], lambda j: fs.at[j], lambda j: fr.at[j])
    fg.start()
    panels = []
    for p in range(1, w):
        c = remote(ct_ref, panel.at[me_w], ps.at[p - 1], pr.at[p - 1], to_wide(lax.rem(me_w + p, w)))
        c.start()
        panels.append(c)
    asks = []
    for p in range(1, n):
        to = lax.rem(me_n + p, n)
        c = remote(ask_ref.at[to], got_ref.at[me_n], qs.at[p - 1], qr.at[p - 1], to_narrow(to))
        c.start()
        asks.append(c)
    local.append(pltpu.make_async_copy(ask_ref.at[me_n], got_ref.at[me_n], loc.at[4]))
    for c in local:
        c.start()

    def bulk(which, c):
        src, dst = ((y_ref, yall_ref), (x_ref, xall_ref))[which]
        first = pl.multiple_of(c * step_rows, step_rows)
        at = pl.ds(first, step_rows)
        send, recv = (lambda j: bs.at[which, c, j]), (lambda j: br.at[which, c, j])
        if n != 8:
            return Gather(n, src.at[at], lambda i: dst.at[i, at], send, recv)
        low = pl.ds(first, step_rows // 2)
        high = pl.ds(pl.multiple_of(first + step_rows // 2, step_rows // 2), step_rows // 2)
        parts = (at, low, high)
        return Relay(src.at[at], lambda i, part: dst.at[i, parts[part]], step_rows, send, recv)

    for c in range(2):
        bulk(0, c).start()
        bulk(1, c).start()
    fg.forward()
    fg.finish()
    for p in range(1, w):
        at = panel.at[lax.rem(me_w + w - p, w)]
        remote(at, at, ps.at[p - 1], pr.at[p - 1], to_wide(lax.rem(me_w + p, w))).wait_recv()
    for c in panels:
        c.wait_send()
    local[0].wait()
    local[1].wait()

    unit = 2.0 * UNIT / features
    half = min(cols, 512)

    def product(i, carry):
        for c in range(cols // half):
            acc = None
            for k in range(w):
                d = lax.dot_general(
                    frag[i, k], panel[k, c * half : (c + 1) * half, :], NT, preferred_element_type=jnp.float32
                )
                acc = d if acc is None else acc + d
            tile[pl.ds(pl.multiple_of(i * rb, rb), rb), c * half : (c + 1) * half] = acc * unit
        return carry

    lax.fori_loop(0, n, product, 0)
    for g in range(cols // BLK):
        sq = jnp.zeros((BLK, 1), jnp.float32)
        for k in range(w):
            v = panel[k, g * BLK : (g + 1) * BLK, :].astype(jnp.float32)
            sq = sq + jnp.sum(v * v, axis=1, keepdims=True)
        bsq[:, g * BLK : (g + 1) * BLK] = as_row(sq, diag) * (UNIT / features)
    gcol[...] = -bsq[...]
    sub = 16
    cg = cols // BLK

    def turn(it, carry):
        g_now = gcol[...]

        def row_group(g, c2):
            ms, zs = [], []
            for s in range(BLK // sub):
                start = pl.multiple_of(g * BLK + s * sub, sub)
                t = tile[pl.ds(start, sub), :] + g_now
                m = jnp.max(t, axis=1, keepdims=True)
                z = jnp.sum(jnp.exp2(t - m), axis=1, keepdims=True)
                ms.append(m)
                zs.append(z)
            whole = jnp.concatenate(ms, axis=0) + jnp.log2(jnp.concatenate(zs, axis=0))
            row_out[it, pl.ds(g, 1), :] = as_row(whole, diag)
            return c2

        lax.fori_loop(0, groups, row_group, 0)
        sent = []
        for p in range(1, n):
            c = remote(
                row_out.at[it],
                row_in.at[it, p - 1],
                rs.at[it, p - 1],
                rr.at[it, p - 1],
                to_narrow(lax.rem(me_n + p, n)),
            )
            c.start()
            sent.append(c)
        bulk(0, it + 2).start()
        for c in sent:
            c.wait_recv()
        top = row_out[it]
        for p in range(n - 1):
            top = jnp.maximum(top, row_in[it, p])
        total = jnp.exp2(row_out[it] - top)
        for p in range(n - 1):
            total = total + jnp.exp2(row_in[it, p] - top)
        frow[...] = jnp.log2(mu_ref[...]) - (top + jnp.log2(total))
        bulk(0, it).forward()

        @pl.when(it >= 1)
        def _():
            bulk(0, it - 1).forward_far()


        def spread(g, c2):
            line = jnp.broadcast_to(frow[pl.ds(g, 1), :], (BLK, BLK))
            frep[pl.ds(pl.multiple_of(g * BLK, BLK), BLK), :] = line.T
            return c2

        lax.fori_loop(0, groups, spread, 0)
        span = 64

        def column_step(r, kept):
            start = pl.multiple_of(r * span, span)
            f = frep[pl.ds(start, span), :]
            out = []
            for c in range(cg):
                old, acc = kept[2 * c], kept[2 * c + 1]
                t = (f + tile[pl.ds(start, span), c * BLK : (c + 1) * BLK]).reshape(span // 8, 8, BLK)
                new = jnp.maximum(old, jnp.max(t, axis=0))
                acc = acc * jnp.exp2(old - new) + jnp.sum(jnp.exp2(t - new[None]), axis=0)
                out += [new, acc]
            return tuple(out)

        begin = (jnp.full((8, BLK), NEG, jnp.float32), jnp.zeros((8, BLK), jnp.float32))
        kept = lax.fori_loop(0, rows // span, column_step, begin * cg)
        for c in range(cg):
            top = jnp.max(kept[2 * c], axis=0, keepdims=True)
            acc = jnp.sum(kept[2 * c + 1] * jnp.exp2(kept[2 * c] - top), axis=0, keepdims=True)
            col_out[it, :, c * BLK : (c + 1) * BLK] = top + jnp.log2(acc)
        csent = []
        for p in range(1, w):
            c = remote(
                col_out.at[it],
                col_in.at[it, p - 1],
                ks.at[it, p - 1],
                kr.at[it, p - 1],
                to_wide(lax.rem(me_w + p, w)),
            )
            c.start()
            csent.append(c)
        bulk(1, it + 2).start()
        for c in csent:
            c.wait_recv()
        top = col_out[it]
        for p in range(w - 1):
            top = jnp.maximum(top, col_in[it, p])
        total = jnp.exp2(col_out[it] - top)
        for p in range(w - 1):
            total = total + jnp.exp2(col_in[it, p] - top)
        gcol[...] = jnp.log2(nu_ref[...]) - (top + jnp.log2(total))
        bulk(1, it).forward()

        @pl.when(it >= 1)
        def _():
            bulk(1, it - 1).forward_far()

        for c in sent:
            c.wait_send()
        for c in csent:
            c.wait_send()
        return carry

    lax.fori_loop(0, ITC, turn, 0)
    gcol[...] = gcol[...] + bsq[...]
    last = []
    for p in range(1, n):
        c = remote(
            gcol, last_in.at[p - 1], ls.at[p - 1], lr.at[p - 1], to_narrow(lax.rem(me_n + p, n))
        )
        c.start()
        last.append(c)
    pot_ref[me_n] = gcol[...]
    for c in last:
        c.wait_recv()
    for p in range(1, n):
        pot_ref[lax.rem(me_n + n - p, n)] = last_in[p - 1]
    for c in last:
        c.wait_send()
    for c in range(ITC, chunks):
        bulk(0, c).forward()
        bulk(1, c).forward()
    for c in range(ITC - 1, chunks):
        bulk(0, c).forward_far()
        bulk(1, c).forward_far()

    def close(c, carry):
        bulk(0, c).finish()
        bulk(1, c).finish()
        return carry

    lax.fori_loop(0, chunks, close, 0)
    for c in local[2:]:
        c.wait()
    for p in range(1, n):
        at = got_ref.at[lax.rem(me_n + n - p, n)]
        remote(at, at, qs.at[p - 1], qr.at[p - 1], to_narrow(lax.rem(me_n + p, n))).wait_recv()
    for c in asks:
        c.wait_send()


def coarse_call(n, w, cs, ct, mu, nu, x, y, asks):
    rb = cs.shape[1]
    cols, part = ct.shape
    rows = rb * n
    groups = rows // BLK
    chunks = ITC + 2
    dma = pltpu.SemaphoreType.DMA
    vm = pl.BlockSpec(memory_space=pltpu.VMEM)
    anyspace = pl.BlockSpec(memory_space=pl.ANY)
    f32 = jnp.float32
    return pl.pallas_call(
        functools.partial(coarse_kernel, n, w),
        out_shape=(
            jax.ShapeDtypeStruct((n, 1, cols), f32),
            jax.ShapeDtypeStruct(asks.shape, asks.dtype),
            jax.ShapeDtypeStruct((n,) + x.shape, x.dtype),
            jax.ShapeDtypeStruct((n,) + y.shape, y.dtype),
        ),
        in_specs=[vm] * 7,
        out_specs=(vm, vm, anyspace, anyspace),
        scratch_shapes=[
            pltpu.VMEM((n, w, rb, part), cs.dtype),
            pltpu.VMEM((w, cols, part), ct.dtype),
            pltpu.VMEM((rows, cols), f32),
            pltpu.VMEM((rows, BLK), f32),
            pltpu.VMEM((groups, BLK), f32),
            pltpu.VMEM((1, cols), f32),
            pltpu.VMEM((1, cols), f32),
            pltpu.VMEM((ITC, groups, BLK), f32),
            pltpu.VMEM((ITC, n - 1, groups, BLK), f32),
            pltpu.VMEM((ITC, 1, cols), f32),
            pltpu.VMEM((ITC, w - 1, 1, cols), f32),
            pltpu.VMEM((n - 1, 1, cols), f32),
            dma((n - 1,)),
            dma((n - 1,)),
            dma((w - 1,)),
            dma((w - 1,)),
            dma((2, chunks, max(n - 1, 8))),
            dma((2, chunks, max(n - 1, 8))),
            dma((ITC, n - 1)),
            dma((ITC, n - 1)),
            dma((ITC, w - 1)),
            dma((ITC, w - 1)),
            dma((n - 1,)),
            dma((n - 1,)),
            dma((n - 1,)),
            dma((n - 1,)),
            dma((5,)),
        ],
        compiler_params=pltpu.CompilerParams(
            collective_id=0, has_side_effects=True, vmem_limit_bytes=VMEM_LIMIT
        ),
        name="coarse",
    )(cs, ct, mu, nu, x, y, asks)


def score_kernel(unit, row_pick, index_ref, own_ref, *refs):
    out = refs[-1]
    step = pl.program_id(0)
    for l in range(GROUP):
        left = own_ref[row_pick(index_ref, step, l)]
        out[l] = lax.dot_general(left, refs[l][0], NT, preferred_element_type=jnp.float32) * unit


def score_call(unit, row_pick, meta, own, pool, entries):
    feature_count = own.shape[-1]

    def pick(l):
        return lambda i, meta_ref: (meta_ref[0, i * GROUP + l], 0, 0)

    return pl.pallas_call(
        functools.partial(score_kernel, unit, row_pick),
        out_shape=jax.ShapeDtypeStruct((entries, BLK, BLK), jnp.float32),
        grid_spec=pltpu.PrefetchScalarGridSpec(
            num_scalar_prefetch=1,
            grid=(entries // GROUP,),
            in_specs=[pl.BlockSpec(own.shape, lambda i, m: (0, 0, 0))]
            + [pl.BlockSpec((1, BLK, feature_count), pick(l)) for l in range(GROUP)],
            out_specs=pl.BlockSpec((GROUP, BLK, BLK), lambda i, m: (i, 0, 0)),
        ),
        compiler_params=pltpu.CompilerParams(vmem_limit_bytes=VMEM_LIMIT),
        name="scores",
    )(meta, own, *([pool] * GROUP))


def fine_kernel(
    n,
    w,
    smeta,
    tmeta,
    ms_ref,
    mt_ref,
    live_ref,
    coarse_ref,
    cl_ref,
    asq_ref,
    bsq_ref,
    fpot_ref,
    gpot_ref,
    ps_ref,
    pt_ref,
    *scratch,
):
    pots = scratch[: 2 * STEPS + 1]
    own_g, mbuf, zbuf, send, recv = scratch[2 * STEPS + 1 :]
    me_n = lax.axis_index("narrow")
    sb = asq_ref.shape[0]
    tb = bsq_ref.shape[0]
    slots = mt_ref.shape[0]
    barrier(n, w)
    diag = diagonal()

    def region(i, count):
        return pl.ds(pl.multiple_of(i * count, count), count)

    def share(x, count):
        for p in range(1, n):
            at = pots[x].at[region(me_n, count)]
            remote(
                at, at, send.at[x, p - 1], recv.at[x, p - 1], to_narrow(lax.rem(me_n + p, n))
            ).start()

    def arrive(x, count):
        for p in range(1, n):
            at = pots[x].at[region(lax.rem(me_n + n - p, n), count)]
            remote(
                at, at, send.at[x, p - 1], recv.at[x, p - 1], to_narrow(lax.rem(me_n + p, n))
            ).wait_recv()
        for p in range(1, n):
            at = pots[x].at[region(me_n, count)]
            remote(
                at, at, send.at[x, p - 1], recv.at[x, p - 1], to_narrow(lax.rem(me_n + p, n))
            ).wait_send()

    points = cl_ref.shape[1]
    hi = coarse_ref.shape[1]
    clusters = cl_ref[...]
    spread = jnp.where(
        lax.broadcasted_iota(jnp.int32, (hi, points), 0) == clusters // BLK, 1.0, 0.0
    ).astype(jnp.float32)
    picked = jnp.dot(
        coarse_ref[...], spread, preferred_element_type=jnp.float32, precision=lax.Precision.HIGHEST
    )
    lane = lax.broadcasted_iota(jnp.int32, (BLK, points), 0) == lax.rem(clusters, BLK)
    begin = jnp.sum(jnp.where(lane, picked, 0.0), axis=0, keepdims=True)
    for b in range(tb):
        pots[0][pl.ds(me_n * tb + b, 1), :] = (
            begin[:, b * BLK : (b + 1) * BLK] - bsq_ref[b : b + 1, :]
        )
    share(0, tb)

    for k in range(STEPS):
        gx = 2 * k
        fx = 2 * k + 1
        nx = 2 * k + 2
        arrive(gx, tb)

        def src_block(b, c2, gx=gx, fx=fx):
            ts = []
            top = None
            for l in range(LIST):
                e = b * LIST + l
                t = ms_ref[e] + pots[gx][pl.ds(smeta[e], 1), :]
                ts.append(t)
                top = t if top is None else jnp.maximum(top, t)
            top = jnp.max(top, axis=1, keepdims=True)
            total = None
            for t in ts:
                v = jnp.exp2(t - top)
                total = v if total is None else total + v
            total = jnp.sum(total, axis=1, keepdims=True)
            pots[fx][pl.ds(me_n * sb + b, 1), :] = as_row(-(top + jnp.log2(total)), diag)
            return c2

        lax.fori_loop(0, sb, src_block, 0, unroll=2)
        share(fx, sb)
        arrive(fx, sb)

        def slot_step(s, c2, fx=fx):
            for u in range(GROUP):
                e = s * GROUP + u
                t = mt_ref[e] + pots[fx][pl.ds(tmeta[0, e], 1), :]
                top = jnp.max(t, axis=1, keepdims=True)
                total = jnp.sum(jnp.exp2(t - top), axis=1, keepdims=True)
                mbuf[pl.ds(e, 1), :] = as_row(top, diag)
                zbuf[pl.ds(e, 1), :] = as_row(total, diag)
            return c2

        lax.fori_loop(0, slots // GROUP, slot_step, 0)
        live = live_ref[...]
        m_all = mbuf[...]
        z_all = zbuf[...]
        for b in range(tb):
            mask = live == b
            top = jnp.max(jnp.where(mask, m_all, NEG), axis=0, keepdims=True)
            part = z_all * jnp.exp2(jnp.where(mask, m_all - top, 0.0))
            total = jnp.sum(jnp.where(mask, part, 0.0), axis=0, keepdims=True)
            line = -(top + jnp.log2(total))
            pots[nx][pl.ds(me_n * tb + b, 1), :] = line
            own_g[b : b + 1, :] = line
        share(nx, tb)

    fx, gx = 2 * STEPS - 1, 2 * STEPS

    def target_plan(s, c2):
        g_line = own_g[pl.ds(tmeta[1, s], 1), :]
        g_col = jnp.broadcast_to(g_line, (BLK, BLK)).T
        t = mt_ref[s] + pots[fx][pl.ds(tmeta[0, s], 1), :] + g_col
        alive = live_ref[pl.ds(s, 1), :] >= 0
        pt_ref[s] = jnp.where(alive, jnp.exp2(t), 0.0).astype(jnp.bfloat16)
        return c2

    lax.fori_loop(0, slots, target_plan, 0)
    fpot_ref[...] = (pots[fx][region(me_n, sb), :] + asq_ref[...]) * (1.0 / UNIT)
    gpot_ref[...] = (own_g[...] + bsq_ref[...]) * (1.0 / UNIT)
    arrive(gx, tb)

    def source_plan(b, c2):
        f_line = pots[fx][pl.ds(me_n * sb + b, 1), :]
        f_col = jnp.broadcast_to(f_line, (BLK, BLK)).T
        for l in range(LIST):
            e = b * LIST + l
            t = ms_ref[e] + pots[gx][pl.ds(smeta[e], 1), :] + f_col
            ps_ref[e] = jnp.exp2(t).astype(jnp.bfloat16)
        return c2

    lax.fori_loop(0, sb, source_plan, 0)


def fine_call(n, w, smeta, tmeta, ms, mt, live, coarse, clusters, asq, bsq):
    vm = pl.BlockSpec(memory_space=pltpu.VMEM)
    sm = pl.BlockSpec(memory_space=pltpu.SMEM)
    dma = pltpu.SemaphoreType.DMA
    f32 = jnp.float32
    turns = 2 * STEPS + 1
    held = n * max(asq.shape[0], bsq.shape[0])
    slots = mt.shape[0]
    return pl.pallas_call(
        functools.partial(fine_kernel, n, w),
        out_shape=(
            jax.ShapeDtypeStruct(asq.shape, f32),
            jax.ShapeDtypeStruct(bsq.shape, f32),
            jax.ShapeDtypeStruct(ms.shape, jnp.bfloat16),
            jax.ShapeDtypeStruct(mt.shape, jnp.bfloat16),
        ),
        in_specs=[sm, sm] + [vm] * 7,
        out_specs=(vm,) * 4,
        scratch_shapes=[
            *[pltpu.VMEM((held, BLK), f32) for _ in range(turns)],
            pltpu.VMEM(bsq.shape, f32),
            pltpu.VMEM((slots, BLK), f32),
            pltpu.VMEM((slots, BLK), f32),
            dma((turns, n - 1)),
            dma((turns, n - 1)),
        ],
        compiler_params=pltpu.CompilerParams(
            collective_id=1, has_side_effects=True, vmem_limit_bytes=VMEM_LIMIT
        ),
        name="fine",
    )(smeta, tmeta, ms, mt, live, coarse, clusters, asq, bsq)


def source_mean_kernel(meta, plan_ref, *refs):
    out = refs[-1]
    num = None
    den = None
    for l in range(LIST):
        p = plan_ref[l]
        d = jnp.dot(p, refs[l][0], preferred_element_type=jnp.float32)
        s = p.astype(jnp.float32)
        num = d if num is None else num + d
        den = s if den is None else den + s
    out[...] = (num / jnp.sum(den, axis=1, keepdims=True)).astype(out.dtype)


def source_mean(meta, plan, pool):
    entries = plan.shape[0]
    feature_count = pool.shape[-1]

    def pick(l):
        return lambda i, m: (m[0, i * LIST + l], 0, 0)

    return pl.pallas_call(
        source_mean_kernel,
        out_shape=jax.ShapeDtypeStruct((entries // LIST * BLK, feature_count), pool.dtype),
        grid_spec=pltpu.PrefetchScalarGridSpec(
            num_scalar_prefetch=1,
            grid=(entries // LIST,),
            in_specs=[pl.BlockSpec((LIST, BLK, BLK), lambda i, m: (i, 0, 0))]
            + [pl.BlockSpec((1, BLK, feature_count), pick(l)) for l in range(LIST)],
            out_specs=pl.BlockSpec((BLK, feature_count), lambda i, m: (i, 0)),
        ),
        compiler_params=pltpu.CompilerParams(vmem_limit_bytes=VMEM_LIMIT),
        name="source_mean",
    )(meta, plan, *([pool] * LIST))


def target_mean_kernel(tb, meta, plan_ref, *refs):
    blocks, (out, num, den) = refs[:GROUP], refs[GROUP:]
    step = pl.program_id(0)

    @pl.when(step == 0)
    def _():
        num[...] = jnp.zeros_like(num)
        den[...] = jnp.zeros_like(den)

    for l in range(GROUP):
        t = meta[1, step * GROUP + l]
        p = plan_ref[l]
        num[t] += jnp.dot(p, blocks[l][0], preferred_element_type=jnp.float32)
        den[t] += p.astype(jnp.float32)

    @pl.when(step == pl.num_programs(0) - 1)
    def _():
        def write(t, carry):
            total = jnp.sum(den[t], axis=1, keepdims=True)
            out[pl.ds(pl.multiple_of(t * BLK, BLK), BLK), :] = (num[t] / total).astype(out.dtype)
            return carry

        lax.fori_loop(0, tb, write, 0)


def target_mean(tb, meta, plan, pool):
    slots = plan.shape[0]
    feature_count = pool.shape[-1]

    def pick(l):
        return lambda i, m: (m[0, i * GROUP + l], 0, 0)

    return pl.pallas_call(
        functools.partial(target_mean_kernel, tb),
        out_shape=jax.ShapeDtypeStruct((tb * BLK, feature_count), pool.dtype),
        grid_spec=pltpu.PrefetchScalarGridSpec(
            num_scalar_prefetch=1,
            grid=(slots // GROUP,),
            in_specs=[pl.BlockSpec((GROUP, BLK, BLK), lambda i, m: (i, 0, 0))]
            + [pl.BlockSpec((1, BLK, feature_count), pick(l)) for l in range(GROUP)],
            out_specs=pl.BlockSpec((tb * BLK, feature_count), lambda i, m: (0, 0)),
            scratch_shapes=[
                pltpu.VMEM((tb, BLK, feature_count), jnp.float32),
                pltpu.VMEM((tb, BLK, BLK), jnp.float32),
            ],
        ),
        compiler_params=pltpu.CompilerParams(vmem_limit_bytes=VMEM_LIMIT),
        name="target_mean",
    )(meta, plan, *([pool] * GROUP))


def square_norms(rows_in):
    return jnp.sum(jnp.square(rows_in.astype(jnp.float32)), axis=-1)


def own_block_of_entry(meta_ref, step, l):
    return step


def own_block_of_slot(meta_ref, step, l):
    return meta_ref[1, step * GROUP + l]


def body(
    sources,
    targets,
    target_lists,
    target_clusters,
    centroids_src,
    centroids_tgt,
    sender_mean_measure,
    recipient_mean_measure,
):
    feature_count = sources.shape[1]
    n = lax.axis_size("narrow")
    w = lax.axis_size("wide")
    sb = sources.shape[0] // BLK
    tb = targets.shape[0] // BLK
    wanted = target_lists.reshape(-1)
    entries = wanted.shape[0]
    capacity = max(
        (5 * sb * LIST + 4 * n - 1) // (4 * n),
        (tb + n - 1) // n,
    )
    slots = n * capacity
    index = jnp.arange(entries, dtype=jnp.int32)
    owner_of = wanted // tb % n
    local_block = wanted % tb
    earlier = jnp.logical_and(owner_of[:, None] == owner_of[None, :], index[None, :] < index[:, None])
    slot_of = owner_of * capacity + jnp.sum(earlier.astype(jnp.int32), axis=1)
    code = local_block + tb * (index // LIST) + 1
    hit = slot_of[None, :] == jnp.arange(slots, dtype=jnp.int32)[:, None]
    requests = jnp.sum(jnp.where(hit, code[None, :], 0), axis=1).reshape(n, capacity)
    cs = centroids_src.reshape(centroids_src.shape[0], w, -1).transpose(1, 0, 2)
    mu = sender_mean_measure.reshape(-1, BLK)
    nu = recipient_mean_measure.reshape(1, -1)
    asks = jnp.pad(requests, ((0, 0), (0, BLK - capacity))).reshape(n, 1, BLK)
    coarse, got, xall, yall = coarse_call(n, w, cs, centroids_tgt, mu, nu, sources, targets, asks)
    asked = got[:, 0, :capacity].reshape(-1) - 1
    alive = asked >= 0
    clipped = jnp.maximum(asked, 0)
    from_block = (jnp.arange(slots, dtype=jnp.int32) // capacity) * sb + clipped // tb
    to_block = clipped % tb
    tmeta = jnp.stack([from_block, to_block])
    live = jnp.broadcast_to(jnp.where(alive, to_block, -1)[:, None], (slots, BLK))
    smeta = owner_of * tb + local_block

    xall = xall.reshape(n * sb, BLK, feature_count)
    yall = yall.reshape(n * tb, BLK, feature_count)
    src_blocks = sources.reshape(sb, BLK, feature_count)
    tgt_blocks = targets.reshape(tb, BLK, feature_count)
    unit = 2.0 * UNIT / feature_count
    ms = score_call(unit, own_block_of_entry, smeta[None, :], src_blocks, yall, entries)
    mt = score_call(unit, own_block_of_slot, tmeta, tgt_blocks, xall, slots)
    asq = square_norms(src_blocks) * (UNIT / feature_count)
    bsq = square_norms(tgt_blocks) * (UNIT / feature_count)
    src_potential, tgt_potential, ps, pt = fine_call(
        n,
        w,
        smeta,
        tmeta,
        ms,
        mt,
        live,
        coarse.reshape(-1, BLK).T,
        target_clusters.reshape(1, -1),
        asq,
        bsq,
    )
    src_bary = source_mean(smeta[None, :], ps, yall)
    tgt_bary = target_mean(tb, tmeta, pt, xall)
    return (src_bary, tgt_bary, src_potential.reshape(-1), tgt_potential.reshape(-1))


def solution(mesh):
    in_specs = (
        P(("wide", "narrow"), None),
        P(("wide", "narrow"), None),
        P(("wide", "narrow"), None),
        P(("wide", "narrow")),
        P(("wide", "narrow"), None),
        P("narrow", "wide"),
        P("wide"),
        P("narrow"),
    )
    out_specs = (
        P(("wide", "narrow"), None),
        P(("wide", "narrow"), None),
        P(("wide", "narrow")),
        P(("wide", "narrow")),
    )
    return jax.shard_map(body, mesh=mesh, in_specs=in_specs, out_specs=out_specs, check_vma=False)
```

```python
import functools
import math

import jax
import jax.numpy as jnp
from jax import lax
from jax.experimental import pallas as pl
from jax.experimental.pallas import tpu as pltpu
from jax.sharding import PartitionSpec as P

BLK = 128
LIST = 4
ITC = 6
STEPS = 3
HEAT = 0.02
LOG2E = math.log2(math.e)
UNIT = LOG2E / HEAT
GROUP = 8
VMEM_LIMIT = 60 * 1024 * 1024
NEG = -jnp.inf
NT = (((1,), (1,)), ((), ()))


def to_narrow(index):
    return {"narrow": index}


def to_wide(index):
    return {"wide": index}


def remote(src, dst, send, recv, target):
    return pltpu.make_async_remote_copy(
        src_ref=src,
        dst_ref=dst,
        send_sem=send,
        recv_sem=recv,
        device_id=target,
        device_id_type=pl.DeviceIdType.MESH,
    )


def barrier(n, w):
    me_n = lax.axis_index("narrow")
    me_w = lax.axis_index("wide")
    sem = pltpu.get_barrier_semaphore()
    for p in range(1, n):
        pl.semaphore_signal(
            sem, inc=1, device_id=to_narrow(lax.rem(me_n + p, n)), device_id_type=pl.DeviceIdType.MESH
        )
    for p in range(1, w):
        pl.semaphore_signal(
            sem, inc=1, device_id=to_wide(lax.rem(me_w + p, w)), device_id_type=pl.DeviceIdType.MESH
        )
    pl.semaphore_wait(sem, n - 1 + w - 1)


class Gather:
    def __init__(self, n, src, slot, send, recv):
        self.n, self.half = n, n // 2
        self.me = lax.axis_index("narrow")
        self.partner = self.me + 1 - 2 * lax.rem(self.me, 2)
        self.src, self.slot, self.send, self.recv = src, slot, send, recv

    def direct(self, p):
        return remote(
            self.src,
            self.slot(self.me),
            self.send(p - 1),
            self.recv(p - 1),
            to_narrow(lax.rem(self.me + 2 * p, self.n)),
        )

    def landed(self, p):
        at = self.slot(lax.rem(self.me + self.n - 2 * p, self.n))
        return remote(
            at, at, self.send(p - 1), self.recv(p - 1), to_narrow(lax.rem(self.me + 2 * p, self.n))
        )

    def own_pair(self):
        j = self.half - 1
        return remote(self.src, self.slot(self.me), self.send(j), self.recv(j), to_narrow(self.partner))

    def passed(self, p):
        j = self.half - 1 + p
        at = self.slot(lax.rem(self.me + self.n - 2 * p, self.n))
        return remote(at, at, self.send(j), self.recv(j), to_narrow(self.partner))

    def start(self):
        for p in range(1, self.half):
            self.direct(p).start()
        self.own_pair().start()

    def forward(self):
        for p in range(1, self.half):
            self.landed(p).wait_recv()
            self.passed(p).start()

    def forward_far(self):
        pass

    def finish(self):
        j = self.half - 1
        at = self.slot(self.partner)
        remote(at, at, self.send(j), self.recv(j), to_narrow(self.partner)).wait_recv()
        for p in range(1, self.half):
            j = self.half - 1 + p
            at = self.slot(lax.rem(self.partner + self.n - 2 * p, self.n))
            remote(at, at, self.send(j), self.recv(j), to_narrow(self.partner)).wait_recv()
        for p in range(1, self.half):
            self.direct(p).wait_send()
        self.own_pair().wait_send()
        for p in range(1, self.half):
            self.passed(p).wait_send()


def flip(index, size):
    return index + size - 2 * size * lax.rem(index // size, 2)


class Relay:
    def __init__(self, src, slot, rows, send, recv):
        me = lax.axis_index("narrow")
        self.me, self.sib, self.xn, self.yn = me, flip(me, 1), flip(me, 2), flip(me, 4)
        self.far = flip(self.xn, 4)
        self.src, self.slot, self.send, self.recv = src, slot, send, recv
        self.low, self.high, self.full = pl.ds(0, rows // 2), pl.ds(rows // 2, rows // 2), pl.ds(0, rows)
        self.rows = rows

    def copy(self, j, src, dst, target):
        return remote(src, dst, self.send(j), self.recv(j), to_narrow(target))

    def through(self, j, owner, part, target):
        at = self.slot(owner, part)
        return self.copy(j, at, at, target)

    def own(self):
        at = self.slot(self.me, 0)
        return [self.copy(j, self.src, at, t) for j, t in enumerate((self.xn, self.yn, self.sib))]

    def relays(self):
        return [
            self.through(3, self.xn, 1, self.yn),
            self.through(4, self.yn, 2, self.xn),
            self.through(5, self.xn, 0, self.sib),
            self.through(6, self.yn, 0, self.sib),
        ]

    def corner(self):
        return self.through(7, self.far, 0, self.sib)

    def start(self):
        for c in self.own():
            c.start()

    def forward(self):
        self.through(0, self.xn, 0, self.xn).wait_recv()
        self.through(1, self.yn, 0, self.yn).wait_recv()
        for c in self.relays():
            c.start()

    def forward_far(self):
        self.through(3, self.far, 1, self.yn).wait_recv()
        self.through(4, self.far, 2, self.xn).wait_recv()
        self.corner().start()

    def finish(self):
        self.through(2, self.sib, 0, self.sib).wait_recv()
        self.through(5, flip(self.sib, 2), 0, self.sib).wait_recv()
        self.through(6, flip(self.sib, 4), 0, self.sib).wait_recv()
        self.through(7, flip(self.far, 1), 0, self.sib).wait_recv()
        for c in self.own() + self.relays() + [self.corner()]:
            c.wait_send()


def diagonal():
    return lax.broadcasted_iota(jnp.int32, (BLK, BLK), 0) == lax.broadcasted_iota(
        jnp.int32, (BLK, BLK), 1
    )


def as_row(column, diag):
    return jnp.sum(jnp.where(diag, column, 0.0), axis=0, keepdims=True)


def coarse_kernel(
    n,
    w,
    cs_ref,
    ct_ref,
    mu_ref,
    nu_ref,
    x_ref,
    y_ref,
    ask_ref,
    pot_ref,
    got_ref,
    xall_ref,
    yall_ref,
    frag,
    panel,
    tile,
    frep,
    frow,
    gcol,
    bsq,
    row_out,
    row_in,
    col_out,
    col_in,
    last_in,
    fs,
    fr,
    ps,
    pr,
    bs,
    br,
    rs,
    rr,
    ks,
    kr,
    ls,
    lr,
    qs,
    qr,
    loc,
):
    me_n = lax.axis_index("narrow")
    me_w = lax.axis_index("wide")
    rb = cs_ref.shape[1]
    cols = ct_ref.shape[0]
    rows = rb * n
    groups = rows // BLK
    features = ct_ref.shape[1] * w
    own_rows = x_ref.shape[0]
    chunks = ITC + 2
    step_rows = own_rows // chunks
    barrier(n, w)
    diag = diagonal()

    local = [
        pltpu.make_async_copy(cs_ref, frag.at[me_n], loc.at[0]),
        pltpu.make_async_copy(ct_ref, panel.at[me_w], loc.at[1]),
        pltpu.make_async_copy(y_ref, yall_ref.at[me_n], loc.at[2]),
        pltpu.make_async_copy(x_ref, xall_ref.at[me_n], loc.at[3]),
    ]
    fg = Gather(n, cs_ref, lambda i: frag.at[i], lambda j: fs.at[j], lambda j: fr.at[j])
    fg.start()
    panels = []
    for p in range(1, w):
        c = remote(ct_ref, panel.at[me_w], ps.at[p - 1], pr.at[p - 1], to_wide(lax.rem(me_w + p, w)))
        c.start()
        panels.append(c)
    asks = []
    for p in range(1, n):
        to = lax.rem(me_n + p, n)
        c = remote(ask_ref.at[to], got_ref.at[me_n], qs.at[p - 1], qr.at[p - 1], to_narrow(to))
        c.start()
        asks.append(c)
    local.append(pltpu.make_async_copy(ask_ref.at[me_n], got_ref.at[me_n], loc.at[4]))
    for c in local:
        c.start()

    def bulk(which, c):
        src, dst = ((y_ref, yall_ref), (x_ref, xall_ref))[which]
        first = pl.multiple_of(c * step_rows, step_rows)
        at = pl.ds(first, step_rows)
        send, recv = (lambda j: bs.at[which, c, j]), (lambda j: br.at[which, c, j])
        if n != 8:
            return Gather(n, src.at[at], lambda i: dst.at[i, at], send, recv)
        low = pl.ds(first, step_rows // 2)
        high = pl.ds(pl.multiple_of(first + step_rows // 2, step_rows // 2), step_rows // 2)
        parts = (at, low, high)
        return Relay(src.at[at], lambda i, part: dst.at[i, parts[part]], step_rows, send, recv)

    ahead = chunks // 2
    for c in range(ahead):
        bulk(0, c).start()
        bulk(1, c).start()
    fg.forward()
    for p in range(1, w):
        at = panel.at[lax.rem(me_w + w - p, w)]
        remote(at, at, ps.at[p - 1], pr.at[p - 1], to_wide(lax.rem(me_w + p, w))).wait_recv()
    local[0].wait()
    local[1].wait()

    unit = 2.0 * UNIT / features
    half = min(cols, 512)

    def product(j, carry, first):
        i = lax.rem(first + 2 * j, n)
        for c in range(cols // half):
            acc = None
            for k in range(w):
                d = lax.dot_general(
                    frag[i, k], panel[k, c * half : (c + 1) * half, :], NT, preferred_element_type=jnp.float32
                )
                acc = d if acc is None else acc + d
            tile[pl.ds(pl.multiple_of(i * rb, rb), rb), c * half : (c + 1) * half] = acc * unit
        return carry

    lax.fori_loop(0, n // 2, functools.partial(product, first=me_n), 0)
    bulk(0, 0).forward()
    bulk(1, 0).forward()
    fg.finish()
    lax.fori_loop(0, n // 2, functools.partial(product, first=fg.partner), 0)
    for c in panels:
        c.wait_send()
    bulk(0, 1).forward()
    bulk(1, 1).forward()
    bulk(0, 0).forward_far()
    bulk(1, 0).forward_far()
    for g in range(cols // BLK):
        sq = jnp.zeros((BLK, 1), jnp.float32)
        for k in range(w):
            v = panel[k, g * BLK : (g + 1) * BLK, :].astype(jnp.float32)
            sq = sq + jnp.sum(v * v, axis=1, keepdims=True)
        bsq[:, g * BLK : (g + 1) * BLK] = as_row(sq, diag) * (UNIT / features)
    gcol[...] = -bsq[...]
    sub = 16
    cg = cols // BLK

    def turn(it, carry):
        g_now = gcol[...]

        def row_group(g, c2):
            ms, zs = [], []
            for s in range(BLK // sub):
                start = pl.multiple_of(g * BLK + s * sub, sub)
                t = tile[pl.ds(start, sub), :] + g_now
                m = jnp.max(t, axis=1, keepdims=True)
                z = jnp.sum(jnp.exp2(t - m), axis=1, keepdims=True)
                ms.append(m)
                zs.append(z)
            whole = jnp.concatenate(ms, axis=0) + jnp.log2(jnp.concatenate(zs, axis=0))
            row_out[it, pl.ds(g, 1), :] = as_row(whole, diag)
            return c2

        lax.fori_loop(0, groups, row_group, 0, unroll=4)
        sent = []
        for p in range(1, n):
            c = remote(
                row_out.at[it],
                row_in.at[it, p - 1],
                rs.at[it, p - 1],
                rr.at[it, p - 1],
                to_narrow(lax.rem(me_n + p, n)),
            )
            c.start()
            sent.append(c)

        @pl.when(it + ahead < chunks)
        def _():
            bulk(0, it + ahead).start()

        for c in sent:
            c.wait_recv()
        top = row_out[it]
        for p in range(n - 1):
            top = jnp.maximum(top, row_in[it, p])
        total = jnp.exp2(row_out[it] - top)
        for p in range(n - 1):
            total = total + jnp.exp2(row_in[it, p] - top)
        frow[...] = jnp.log2(mu_ref[...]) - (top + jnp.log2(total))
        bulk(0, it + 2).forward()
        bulk(0, it + 1).forward_far()


        def spread(g, c2):
            line = jnp.broadcast_to(frow[pl.ds(g, 1), :], (BLK, BLK))
            frep[pl.ds(pl.multiple_of(g * BLK, BLK), BLK), :] = line.T
            return c2

        lax.fori_loop(0, groups, spread, 0, unroll=4)
        span = 64

        def column_step(r, kept):
            start = pl.multiple_of(r * span, span)
            f = frep[pl.ds(start, span), :]
            out = []
            for c in range(cg):
                old, acc = kept[2 * c], kept[2 * c + 1]
                t = (f + tile[pl.ds(start, span), c * BLK : (c + 1) * BLK]).reshape(span // 8, 8, BLK)
                new = jnp.maximum(old, jnp.max(t, axis=0))
                acc = acc * jnp.exp2(old - new) + jnp.sum(jnp.exp2(t - new[None]), axis=0)
                out += [new, acc]
            return tuple(out)

        begin = (jnp.full((8, BLK), NEG, jnp.float32), jnp.zeros((8, BLK), jnp.float32))
        kept = lax.fori_loop(0, rows // span, column_step, begin * cg)
        for c in range(cg):
            top = jnp.max(kept[2 * c], axis=0, keepdims=True)
            acc = jnp.sum(kept[2 * c + 1] * jnp.exp2(kept[2 * c] - top), axis=0, keepdims=True)
            col_out[it, :, c * BLK : (c + 1) * BLK] = top + jnp.log2(acc)
        csent = []
        for p in range(1, w):
            c = remote(
                col_out.at[it],
                col_in.at[it, p - 1],
                ks.at[it, p - 1],
                kr.at[it, p - 1],
                to_wide(lax.rem(me_w + p, w)),
            )
            c.start()
            csent.append(c)

        @pl.when(it + ahead < chunks)
        def _():
            bulk(1, it + ahead).start()

        for c in csent:
            c.wait_recv()
        top = col_out[it]
        for p in range(w - 1):
            top = jnp.maximum(top, col_in[it, p])
        total = jnp.exp2(col_out[it] - top)
        for p in range(w - 1):
            total = total + jnp.exp2(col_in[it, p] - top)
        gcol[...] = jnp.log2(nu_ref[...]) - (top + jnp.log2(total))
        bulk(1, it + 2).forward()
        bulk(1, it + 1).forward_far()

        for c in sent:
            c.wait_send()
        for c in csent:
            c.wait_send()
        return carry

    lax.fori_loop(0, ITC, turn, 0)
    gcol[...] = gcol[...] + bsq[...]
    last = []
    for p in range(1, n):
        c = remote(
            gcol, last_in.at[p - 1], ls.at[p - 1], lr.at[p - 1], to_narrow(lax.rem(me_n + p, n))
        )
        c.start()
        last.append(c)
    pot_ref[me_n] = gcol[...]
    for c in last:
        c.wait_recv()
    for p in range(1, n):
        pot_ref[lax.rem(me_n + n - p, n)] = last_in[p - 1]
    for c in last:
        c.wait_send()
    bulk(0, chunks - 1).forward_far()
    bulk(1, chunks - 1).forward_far()

    def close(c, carry):
        bulk(0, c).finish()
        bulk(1, c).finish()
        return carry

    lax.fori_loop(0, chunks, close, 0)
    for c in local[2:]:
        c.wait()
    for p in range(1, n):
        at = got_ref.at[lax.rem(me_n + n - p, n)]
        remote(at, at, qs.at[p - 1], qr.at[p - 1], to_narrow(lax.rem(me_n + p, n))).wait_recv()
    for c in asks:
        c.wait_send()


def coarse_call(n, w, cs, ct, mu, nu, x, y, asks):
    rb = cs.shape[1]
    cols, part = ct.shape
    rows = rb * n
    groups = rows // BLK
    chunks = ITC + 2
    dma = pltpu.SemaphoreType.DMA
    vm = pl.BlockSpec(memory_space=pltpu.VMEM)
    anyspace = pl.BlockSpec(memory_space=pl.ANY)
    f32 = jnp.float32
    return pl.pallas_call(
        functools.partial(coarse_kernel, n, w),
        out_shape=(
            jax.ShapeDtypeStruct((n, 1, cols), f32),
            jax.ShapeDtypeStruct(asks.shape, asks.dtype),
            jax.ShapeDtypeStruct((n,) + x.shape, x.dtype),
            jax.ShapeDtypeStruct((n,) + y.shape, y.dtype),
        ),
        in_specs=[vm] * 7,
        out_specs=(vm, vm, anyspace, anyspace),
        scratch_shapes=[
            pltpu.VMEM((n, w, rb, part), cs.dtype),
            pltpu.VMEM((w, cols, part), ct.dtype),
            pltpu.VMEM((rows, cols), f32),
            pltpu.VMEM((rows, BLK), f32),
            pltpu.VMEM((groups, BLK), f32),
            pltpu.VMEM((1, cols), f32),
            pltpu.VMEM((1, cols), f32),
            pltpu.VMEM((ITC, groups, BLK), f32),
            pltpu.VMEM((ITC, n - 1, groups, BLK), f32),
            pltpu.VMEM((ITC, 1, cols), f32),
            pltpu.VMEM((ITC, w - 1, 1, cols), f32),
            pltpu.VMEM((n - 1, 1, cols), f32),
            dma((n - 1,)),
            dma((n - 1,)),
            dma((w - 1,)),
            dma((w - 1,)),
            dma((2, chunks, max(n - 1, 8))),
            dma((2, chunks, max(n - 1, 8))),
            dma((ITC, n - 1)),
            dma((ITC, n - 1)),
            dma((ITC, w - 1)),
            dma((ITC, w - 1)),
            dma((n - 1,)),
            dma((n - 1,)),
            dma((n - 1,)),
            dma((n - 1,)),
            dma((5,)),
        ],
        compiler_params=pltpu.CompilerParams(
            collective_id=0, has_side_effects=True, vmem_limit_bytes=VMEM_LIMIT
        ),
        name="coarse",
    )(cs, ct, mu, nu, x, y, asks)


def score_kernel(unit, row_pick, index_ref, own_ref, *refs):
    out = refs[-1]
    step = pl.program_id(0)
    for l in range(GROUP):
        left = own_ref[row_pick(index_ref, step, l)]
        out[l] = lax.dot_general(left, refs[l][0], NT, preferred_element_type=jnp.float32) * unit


def score_call(unit, row_pick, meta, own, pool, entries):
    feature_count = own.shape[-1]

    def pick(l):
        return lambda i, meta_ref: (meta_ref[0, i * GROUP + l], 0, 0)

    return pl.pallas_call(
        functools.partial(score_kernel, unit, row_pick),
        out_shape=jax.ShapeDtypeStruct((entries, BLK, BLK), jnp.float32),
        grid_spec=pltpu.PrefetchScalarGridSpec(
            num_scalar_prefetch=1,
            grid=(entries // GROUP,),
            in_specs=[pl.BlockSpec(own.shape, lambda i, m: (0, 0, 0))]
            + [pl.BlockSpec((1, BLK, feature_count), pick(l)) for l in range(GROUP)],
            out_specs=pl.BlockSpec((GROUP, BLK, BLK), lambda i, m: (i, 0, 0)),
        ),
        compiler_params=pltpu.CompilerParams(vmem_limit_bytes=VMEM_LIMIT),
        name="scores",
    )(meta, own, *([pool] * GROUP))


def fine_kernel(
    n,
    w,
    smeta,
    tmeta,
    ms_ref,
    mt_ref,
    live_ref,
    coarse_ref,
    cl_ref,
    asq_ref,
    bsq_ref,
    fpot_ref,
    gpot_ref,
    ps_ref,
    pt_ref,
    *scratch,
):
    pots = scratch[: 2 * STEPS + 1]
    own_g, mbuf, zbuf, send, recv = scratch[2 * STEPS + 1 :]
    me_n = lax.axis_index("narrow")
    sb = asq_ref.shape[0]
    tb = bsq_ref.shape[0]
    slots = mt_ref.shape[0]
    barrier(n, w)
    diag = diagonal()

    def region(i, count):
        return pl.ds(pl.multiple_of(i * count, count), count)

    def share(x, count):
        for p in range(1, n):
            at = pots[x].at[region(me_n, count)]
            remote(
                at, at, send.at[x, p - 1], recv.at[x, p - 1], to_narrow(lax.rem(me_n + p, n))
            ).start()

    def arrive(x, count):
        for p in range(1, n):
            at = pots[x].at[region(lax.rem(me_n + n - p, n), count)]
            remote(
                at, at, send.at[x, p - 1], recv.at[x, p - 1], to_narrow(lax.rem(me_n + p, n))
            ).wait_recv()
        for p in range(1, n):
            at = pots[x].at[region(me_n, count)]
            remote(
                at, at, send.at[x, p - 1], recv.at[x, p - 1], to_narrow(lax.rem(me_n + p, n))
            ).wait_send()

    points = cl_ref.shape[1]
    hi = coarse_ref.shape[1]
    clusters = cl_ref[...]
    spread = jnp.where(
        lax.broadcasted_iota(jnp.int32, (hi, points), 0) == clusters // BLK, 1.0, 0.0
    ).astype(jnp.float32)
    picked = jnp.dot(
        coarse_ref[...], spread, preferred_element_type=jnp.float32, precision=lax.Precision.HIGHEST
    )
    lane = lax.broadcasted_iota(jnp.int32, (BLK, points), 0) == lax.rem(clusters, BLK)
    begin = jnp.sum(jnp.where(lane, picked, 0.0), axis=0, keepdims=True)
    for b in range(tb):
        pots[0][pl.ds(me_n * tb + b, 1), :] = (
            begin[:, b * BLK : (b + 1) * BLK] - bsq_ref[b : b + 1, :]
        )
    share(0, tb)

    for k in range(STEPS):
        gx = 2 * k
        fx = 2 * k + 1
        nx = 2 * k + 2
        arrive(gx, tb)

        def src_block(b, c2, gx=gx, fx=fx):
            ts = []
            top = None
            for l in range(LIST):
                e = b * LIST + l
                t = ms_ref[e] + pots[gx][pl.ds(smeta[e], 1), :]
                ts.append(t)
                top = t if top is None else jnp.maximum(top, t)
            top = jnp.max(top, axis=1, keepdims=True)
            total = None
            for t in ts:
                v = jnp.exp2(t - top)
                total = v if total is None else total + v
            total = jnp.sum(total, axis=1, keepdims=True)
            pots[fx][pl.ds(me_n * sb + b, 1), :] = as_row(-(top + jnp.log2(total)), diag)
            return c2

        lax.fori_loop(0, sb, src_block, 0, unroll=4)
        share(fx, sb)
        arrive(fx, sb)

        def slot_step(s, c2, fx=fx):
            for u in range(GROUP):
                e = s * GROUP + u
                t = mt_ref[e] + pots[fx][pl.ds(tmeta[0, e], 1), :]
                top = jnp.max(t, axis=1, keepdims=True)
                total = jnp.sum(jnp.exp2(t - top), axis=1, keepdims=True)
                mbuf[pl.ds(e, 1), :] = as_row(top, diag)
                zbuf[pl.ds(e, 1), :] = as_row(total, diag)
            return c2

        lax.fori_loop(0, slots // GROUP, slot_step, 0)
        live = live_ref[...]
        m_all = mbuf[...]
        z_all = zbuf[...]
        for b in range(tb):
            mask = live == b
            top = jnp.max(jnp.where(mask, m_all, NEG), axis=0, keepdims=True)
            part = z_all * jnp.exp2(jnp.where(mask, m_all - top, 0.0))
            total = jnp.sum(jnp.where(mask, part, 0.0), axis=0, keepdims=True)
            line = -(top + jnp.log2(total))
            pots[nx][pl.ds(me_n * tb + b, 1), :] = line
            own_g[b : b + 1, :] = line
        share(nx, tb)

    fx, gx = 2 * STEPS - 1, 2 * STEPS

    def target_plan(s, c2):
        g_line = own_g[pl.ds(tmeta[1, s], 1), :]
        g_col = jnp.broadcast_to(g_line, (BLK, BLK)).T
        t = mt_ref[s] + pots[fx][pl.ds(tmeta[0, s], 1), :] + g_col
        alive = live_ref[pl.ds(s, 1), :] >= 0
        pt_ref[s] = jnp.where(alive, jnp.exp2(t), 0.0).astype(jnp.bfloat16)
        return c2

    lax.fori_loop(0, slots, target_plan, 0, unroll=4)
    fpot_ref[...] = (pots[fx][region(me_n, sb), :] + asq_ref[...]) * (1.0 / UNIT)
    gpot_ref[...] = (own_g[...] + bsq_ref[...]) * (1.0 / UNIT)
    arrive(gx, tb)

    def source_plan(b, c2):
        f_line = pots[fx][pl.ds(me_n * sb + b, 1), :]
        f_col = jnp.broadcast_to(f_line, (BLK, BLK)).T
        for l in range(LIST):
            e = b * LIST + l
            t = ms_ref[e] + pots[gx][pl.ds(smeta[e], 1), :] + f_col
            ps_ref[e] = jnp.exp2(t).astype(jnp.bfloat16)
        return c2

    lax.fori_loop(0, sb, source_plan, 0, unroll=2)


def fine_call(n, w, smeta, tmeta, ms, mt, live, coarse, clusters, asq, bsq):
    vm = pl.BlockSpec(memory_space=pltpu.VMEM)
    sm = pl.BlockSpec(memory_space=pltpu.SMEM)
    dma = pltpu.SemaphoreType.DMA
    f32 = jnp.float32
    turns = 2 * STEPS + 1
    held = n * max(asq.shape[0], bsq.shape[0])
    slots = mt.shape[0]
    return pl.pallas_call(
        functools.partial(fine_kernel, n, w),
        out_shape=(
            jax.ShapeDtypeStruct(asq.shape, f32),
            jax.ShapeDtypeStruct(bsq.shape, f32),
            jax.ShapeDtypeStruct(ms.shape, jnp.bfloat16),
            jax.ShapeDtypeStruct(mt.shape, jnp.bfloat16),
        ),
        in_specs=[sm, sm] + [vm] * 7,
        out_specs=(vm,) * 4,
        scratch_shapes=[
            *[pltpu.VMEM((held, BLK), f32) for _ in range(turns)],
            pltpu.VMEM(bsq.shape, f32),
            pltpu.VMEM((slots, BLK), f32),
            pltpu.VMEM((slots, BLK), f32),
            dma((turns, n - 1)),
            dma((turns, n - 1)),
        ],
        compiler_params=pltpu.CompilerParams(
            collective_id=1, has_side_effects=True, vmem_limit_bytes=VMEM_LIMIT
        ),
        name="fine",
    )(smeta, tmeta, ms, mt, live, coarse, clusters, asq, bsq)


def source_mean_kernel(meta, plan_ref, *refs):
    out = refs[-1]
    num = None
    den = None
    for l in range(LIST):
        p = plan_ref[l]
        d = jnp.dot(p, refs[l][0], preferred_element_type=jnp.float32)
        s = p.astype(jnp.float32)
        num = d if num is None else num + d
        den = s if den is None else den + s
    out[...] = (num / jnp.sum(den, axis=1, keepdims=True)).astype(out.dtype)


def source_mean(meta, plan, pool):
    entries = plan.shape[0]
    feature_count = pool.shape[-1]

    def pick(l):
        return lambda i, m: (m[0, i * LIST + l], 0, 0)

    return pl.pallas_call(
        source_mean_kernel,
        out_shape=jax.ShapeDtypeStruct((entries // LIST * BLK, feature_count), pool.dtype),
        grid_spec=pltpu.PrefetchScalarGridSpec(
            num_scalar_prefetch=1,
            grid=(entries // LIST,),
            in_specs=[pl.BlockSpec((LIST, BLK, BLK), lambda i, m: (i, 0, 0))]
            + [pl.BlockSpec((1, BLK, feature_count), pick(l)) for l in range(LIST)],
            out_specs=pl.BlockSpec((BLK, feature_count), lambda i, m: (i, 0)),
        ),
        compiler_params=pltpu.CompilerParams(vmem_limit_bytes=VMEM_LIMIT),
        name="source_mean",
    )(meta, plan, *([pool] * LIST))


def target_mean_kernel(tb, meta, plan_ref, *refs):
    blocks, (out, num, den) = refs[:GROUP], refs[GROUP:]
    step = pl.program_id(0)

    @pl.when(step == 0)
    def _():
        num[...] = jnp.zeros_like(num)
        den[...] = jnp.zeros_like(den)

    for l in range(GROUP):
        t = meta[1, step * GROUP + l]
        p = plan_ref[l]
        num[t] += jnp.dot(p, blocks[l][0], preferred_element_type=jnp.float32)
        den[t] += p.astype(jnp.float32)

    @pl.when(step == pl.num_programs(0) - 1)
    def _():
        def write(t, carry):
            total = jnp.sum(den[t], axis=1, keepdims=True)
            out[pl.ds(pl.multiple_of(t * BLK, BLK), BLK), :] = (num[t] / total).astype(out.dtype)
            return carry

        lax.fori_loop(0, tb, write, 0)


def target_mean(tb, meta, plan, pool):
    slots = plan.shape[0]
    feature_count = pool.shape[-1]

    def pick(l):
        return lambda i, m: (m[0, i * GROUP + l], 0, 0)

    return pl.pallas_call(
        functools.partial(target_mean_kernel, tb),
        out_shape=jax.ShapeDtypeStruct((tb * BLK, feature_count), pool.dtype),
        grid_spec=pltpu.PrefetchScalarGridSpec(
            num_scalar_prefetch=1,
            grid=(slots // GROUP,),
            in_specs=[pl.BlockSpec((GROUP, BLK, BLK), lambda i, m: (i, 0, 0))]
            + [pl.BlockSpec((1, BLK, feature_count), pick(l)) for l in range(GROUP)],
            out_specs=pl.BlockSpec((tb * BLK, feature_count), lambda i, m: (0, 0)),
            scratch_shapes=[
                pltpu.VMEM((tb, BLK, feature_count), jnp.float32),
                pltpu.VMEM((tb, BLK, BLK), jnp.float32),
            ],
        ),
        compiler_params=pltpu.CompilerParams(vmem_limit_bytes=VMEM_LIMIT),
        name="target_mean",
    )(meta, plan, *([pool] * GROUP))


def square_norms(rows_in):
    return jnp.sum(jnp.square(rows_in.astype(jnp.float32)), axis=-1)


def own_block_of_entry(meta_ref, step, l):
    return (step * GROUP + l) // LIST


def own_block_of_slot(meta_ref, step, l):
    return meta_ref[1, step * GROUP + l]


def body(
    sources,
    targets,
    target_lists,
    target_clusters,
    centroids_src,
    centroids_tgt,
    sender_mean_measure,
    recipient_mean_measure,
):
    feature_count = sources.shape[1]
    n = lax.axis_size("narrow")
    w = lax.axis_size("wide")
    sb = sources.shape[0] // BLK
    tb = targets.shape[0] // BLK
    wanted = target_lists.reshape(-1)
    entries = wanted.shape[0]
    capacity = max(
        (5 * sb * LIST + 4 * n - 1) // (4 * n),
        (tb + n - 1) // n,
    )
    slots = n * capacity
    index = jnp.arange(entries, dtype=jnp.int32)
    owner_of = wanted // tb % n
    local_block = wanted % tb
    earlier = jnp.logical_and(owner_of[:, None] == owner_of[None, :], index[None, :] < index[:, None])
    slot_of = owner_of * capacity + jnp.sum(earlier.astype(jnp.int32), axis=1)
    code = local_block + tb * (index // LIST) + 1
    hit = slot_of[None, :] == jnp.arange(slots, dtype=jnp.int32)[:, None]
    requests = jnp.sum(jnp.where(hit, code[None, :], 0), axis=1).reshape(n, capacity)
    cs = centroids_src.reshape(centroids_src.shape[0], w, -1).transpose(1, 0, 2)
    mu = sender_mean_measure.reshape(-1, BLK)
    nu = recipient_mean_measure.reshape(1, -1)
    asks = jnp.pad(requests, ((0, 0), (0, BLK - capacity))).reshape(n, 1, BLK)
    coarse, got, xall, yall = coarse_call(n, w, cs, centroids_tgt, mu, nu, sources, targets, asks)
    asked = got[:, 0, :capacity].reshape(-1) - 1
    alive = asked >= 0
    clipped = jnp.maximum(asked, 0)
    from_block = (jnp.arange(slots, dtype=jnp.int32) // capacity) * sb + clipped // tb
    to_block = clipped % tb
    tmeta = jnp.stack([from_block, to_block])
    live = jnp.broadcast_to(jnp.where(alive, to_block, -1)[:, None], (slots, BLK))
    smeta = owner_of * tb + local_block

    xall = xall.reshape(n * sb, BLK, feature_count)
    yall = yall.reshape(n * tb, BLK, feature_count)
    src_blocks = sources.reshape(sb, BLK, feature_count)
    tgt_blocks = targets.reshape(tb, BLK, feature_count)
    unit = 2.0 * UNIT / feature_count
    ms = score_call(unit, own_block_of_entry, smeta[None, :], src_blocks, yall, entries)
    mt = score_call(unit, own_block_of_slot, tmeta, tgt_blocks, xall, slots)
    asq = square_norms(src_blocks) * (UNIT / feature_count)
    bsq = square_norms(tgt_blocks) * (UNIT / feature_count)
    src_potential, tgt_potential, ps, pt = fine_call(
        n,
        w,
        smeta,
        tmeta,
        ms,
        mt,
        live,
        coarse.reshape(-1, BLK).T,
        target_clusters.reshape(1, -1),
        asq,
        bsq,
    )
    src_bary = source_mean(smeta[None, :], ps, yall)
    tgt_bary = target_mean(tb, tmeta, pt, xall)
    return (src_bary, tgt_bary, src_potential.reshape(-1), tgt_potential.reshape(-1))


def solution(mesh):
    in_specs = (
        P(("wide", "narrow"), None),
        P(("wide", "narrow"), None),
        P(("wide", "narrow"), None),
        P(("wide", "narrow")),
        P(("wide", "narrow"), None),
        P("narrow", "wide"),
        P("wide"),
        P("narrow"),
    )
    out_specs = (
        P(("wide", "narrow"), None),
        P(("wide", "narrow"), None),
        P(("wide", "narrow")),
        P(("wide", "narrow")),
    )
    return jax.shard_map(body, mesh=mesh, in_specs=in_specs, out_specs=out_specs, check_vma=False)
```
